512 devices in a mesh: px: 16 (over z, core), py: 32 (over x, y).
Axes of the slice: x: 4, y: 8, z: 8, core: 2. Of those that a mesh axis runs over, the one named last changes fastest.
Arguments:
- field_in: bfloat16 [32, 32, 512, 512], P(None, 'py', 'px'), may hold values from -6 to 6
- cotangent: bfloat16 [32, 32, 512, 512], P(None, 'py', 'px'), may hold values from -6 to 6
- spectrum_saved: float32 [32, 32, 32, 32, 2], P(None, None, 'px', 'py'), may hold values from -6 to 6
- weight_store: float32 [2048, 2, 32, 32], P(('px', 'py')), may hold values from -4.2 to 4.2
- block_slot: int32 [32, 32], P('py', 'px'), may hold values from 0 to 127, as said below
- kx_modes: int32 [32], replicated, may hold values from 0 to 511, as said below
- ky_modes: int32 [32], replicated, may hold values from 0 to 511, as said below
- pointwise: bfloat16 [32, 32], replicated, may hold values from -0.25 to 0.25
- bias_vector: float32 [32], replicated, may hold values from -3 to 3
Outputs:
- field_grad: float32 [32, 32, 512, 512], P(None, 'py', 'px')
- store_grad: float32 [2048, 2, 32, 32], P(('px', 'py'))
The draws below stay inside these ranges and needn't reach their ends.
Inputs may be any that keep to these rules, and one draw needn't show every extreme that they name: `kx_modes`: 32 distinct wave numbers k, each with k < 32 or k > 480. `ky_modes`: 32 distinct wave numbers k, each with k < 32 or k > 480. `block_slot`: within each px index's 2 second-dimension modes, the values over all 32 x 2 mode pairs are distinct; v // 4 is the py index of the device that stores the block and v % 4 its slot there; in each such group one py index stores 4 blocks, and the other slots hold unused blocks.
All inputs are finite; a program needn't handle non-finite values.
Results may differ from the reference program's by a relative error of at most 0.0003.
Values sent between devices are 32-bit elements; how exact they have to be, the bound alone decides.
A program may use at most 64 MiB of HBM per device.

```python
import math
import jax
import jax.numpy as jnp
from jax import lax

C = 32
NX = 512
NY = 512
MX = 32
MY = 32
NZ = 32
MY_DEV = 2
CAP = 4
ROW_SLOTS = 128
STORE = 2048
N_PX = 16
N_PY = 32


def low_modes(key, count, length):
    picks = jax.random.permutation(key, 2 * count - 1).astype(jnp.int32)[:count]
    return jnp.where(picks < count, picks, length - (picks - count + 1)).astype(jnp.int32)


def draw_kx_modes(key, part):
    return low_modes(jax.random.fold_in(key, 11), MX, NX)


def draw_ky_modes(key, part):
    return low_modes(jax.random.fold_in(key, 23), MY, NY)


def draw_block_slot(key, part):
    rows_y = MY // N_PX
    count = MX * rows_y
    keys = jax.random.split(jax.random.fold_in(key, 37), N_PX)
    row_ids = jnp.arange(N_PX, dtype=jnp.int32)

    def one_row(row_key, row_id):
        key_order, key_busy = jax.random.split(row_key)
        order = jax.random.permutation(key_order, count).astype(jnp.int32)
        drawn = jax.random.randint(key_busy, (), 0, N_PY).astype(jnp.int32)
        busy = jnp.where(row_id == 0, N_PY - 1, drawn).astype(jnp.int32)
        place = jnp.arange(count, dtype=jnp.int32)
        others = place - CAP
        owner = jnp.where(place < CAP, busy, (busy + 1 + others % (N_PY - 1)) % N_PY)
        slot = jnp.where(place < CAP, place, others // (N_PY - 1))
        return jnp.zeros((count,), jnp.int32).at[order].set((owner * CAP + slot).astype(jnp.int32))
    table = jax.vmap(one_row)(keys, row_ids)
    return jnp.transpose(table.reshape(N_PX, MX, rows_y), (1, 0, 2)).reshape(MX, MY).astype(jnp.int32)


def levels(own_key, dims, shards, least, high):
    def one(axis_at, shards_of):
        draws = jax.random.uniform(jax.random.fold_in(jax.random.fold_in(own_key, 6), axis_at), (shards_of,), jnp.float32, least / len(shards), high / len(shards))
        return jnp.repeat(jnp.exp(draws), dims[axis_at] // shards_of).reshape((-1,) + (1,) * (len(dims) - axis_at - 1))

    factor_of = one(*shards[0])
    for cut in shards[1:]:
        factor_of = factor_of * one(*cut)
    return factor_of


def bell_draw(rng, shape, width, most, shards=(), held_as=jnp.bfloat16):
    values = jax.random.normal(rng, shape, jnp.float32) * width
    if len(shards) > 0:
        values = levels(rng, shape, shards, -0.22, 0.18) * values
    return jnp.clip(values, min=-most, max=most).astype(held_as)


def setup_inputs(seed: int = 0) -> dict:
    key_of = jax.random.split(jax.random.key(seed), 10)
    return {
        "field_in": bell_draw(key_of[0], (C, NZ, NX, NY), 1.0, 6.0, ((1, 32), (2, 16))),
        "cotangent": bell_draw(key_of[1], (C, NZ, NX, NY), 1.0, 6.0, ((1, 32), (2, 16))),
        "spectrum_saved": bell_draw(key_of[2], (C, NZ, MY, MX, 2), 1.0, 6.0, ((2, 16), (3, 32)), jnp.float32),
        "weight_store": bell_draw(key_of[3], (STORE, 2, C, C), 0.7, 4.2, ((0, 512),), jnp.float32),
        "block_slot": draw_block_slot(jax.random.fold_in(key_of[9], 71), 0),
        "kx_modes": draw_kx_modes(jax.random.fold_in(key_of[9], 71), 0),
        "ky_modes": draw_ky_modes(jax.random.fold_in(key_of[9], 71), 0),
        "pointwise": bell_draw(key_of[7], (C, C), (16 * C) ** -0.5, 0.25),
        "bias_vector": bell_draw(key_of[8], (C,), 0.5, 3.0, (), jnp.float32),
    }


precise = lax.Precision.HIGHEST

def gelu_slope(values):
    normal_cdf = 0.5 * (1.0 + lax.erf(values * 0.7071067811865476))
    density = jnp.exp(-0.5 * values * values) * 0.3989422804014327
    return normal_cdf + values * density

def reference(field_in, cotangent, spectrum_saved, weight_store, block_slot, kx_modes, ky_modes, pointwise, bias_vector):
    row_of = jnp.arange(MY, dtype=jnp.int32) // MY_DEV
    indices = (row_of[None, :] * ROW_SLOTS + block_slot).astype(jnp.int32)
    blocks = jnp.take(weight_store, indices.reshape(-1), axis=0).reshape(MX, MY, 2, C, C)
    block_re = blocks[:, :, 0]
    block_im = blocks[:, :, 1]
    factor = 1.0 / math.sqrt(NX * NY)
    weight_full = pointwise.astype(jnp.float32)
    rows_x = kx_modes[:, None]
    cols_y = ky_modes[None, :]

    def plane(total, depth):
        values = lax.dynamic_index_in_dim(field_in, depth, 1, False).astype(jnp.float32)
        upstream = lax.dynamic_index_in_dim(cotangent, depth, 1, False).astype(jnp.float32)
        saved = lax.dynamic_index_in_dim(spectrum_saved, depth, 1, False)
        spec_re = jnp.transpose(saved[..., 0], (0, 2, 1))
        spec_im = jnp.transpose(saved[..., 1], (0, 2, 1))
        form = 'aboc,cab->oab'
        mixed_re = jnp.einsum(form, block_re, spec_re, precision=precise) - jnp.einsum(form, block_im, spec_im, precision=precise)
        mixed_im = jnp.einsum(form, block_re, spec_im, precision=precise) + jnp.einsum(form, block_im, spec_re, precision=precise)
        base = jnp.zeros_like(values)
        full = lax.complex(base.at[:, rows_x, cols_y].set(mixed_re), base.at[:, rows_x, cols_y].set(mixed_im))
        spectral = jnp.real(jnp.fft.ifft2(full, axes=(1, 2))) * (NX * NY * factor)
        pre = jnp.einsum('oc,cxy->oxy', weight_full, values, precision=precise) + bias_vector[:, None, None] + spectral
        grad = upstream * gelu_slope(pre)
        transform = jnp.fft.fft2(grad, axes=(1, 2))[:, rows_x, cols_y] * factor
        grad_re = jnp.real(transform)
        grad_im = jnp.imag(transform)
        back_form = 'aboc,oab->cab'
        adj_re = jnp.einsum(back_form, block_re, grad_re, precision=precise) + jnp.einsum(back_form, block_im, grad_im, precision=precise)
        adj_im = jnp.einsum(back_form, block_re, grad_im, precision=precise) - jnp.einsum(back_form, block_im, grad_re, precision=precise)
        back = lax.complex(base.at[:, rows_x, cols_y].set(adj_re), base.at[:, rows_x, cols_y].set(adj_im))
        plane_grad = jnp.einsum('oc,oxy->cxy', weight_full, grad, precision=precise)
        plane_grad = plane_grad + jnp.real(jnp.fft.ifft2(back, axes=(1, 2))) * (NX * NY * factor)
        grad_form = 'oab,cab->aboc'
        step_re = jnp.einsum(grad_form, grad_re, spec_re, precision=precise) + jnp.einsum(grad_form, grad_im, spec_im, precision=precise)
        step_im = jnp.einsum(grad_form, grad_im, spec_re, precision=precise) - jnp.einsum(grad_form, grad_re, spec_im, precision=precise)
        return (total + jnp.stack([step_re, step_im], 2), plane_grad)
    start = jnp.zeros((MX, MY, 2, C, C), jnp.float32)
    total, grads = lax.scan(plane, start, jnp.arange(NZ, dtype=jnp.int32))
    field_grad = jnp.moveaxis(grads, 0, 1)
    store_grad = jnp.zeros_like(weight_store).at[indices.reshape(-1)].set(total.reshape(MX * MY, 2, C, C))
    return (field_grad, store_grad)
```

```python
import math

import jax
import jax.numpy as jnp
from jax import lax
from jax.sharding import PartitionSpec as P

precise = lax.Precision.HIGHEST


def phase_table(length, modes):
    points = lax.iota(jnp.int32, length)
    wrapped = points[:, None] * modes[None, :] % length
    angle = wrapped.astype(jnp.float32) * (2.0 * math.pi / length)
    return (jnp.cos(angle), jnp.sin(angle))


def gelu_slope(values):
    normal_cdf = 0.5 * (1.0 + lax.erf(values * 0.7071067811865476))
    density = jnp.exp(-0.5 * values * values) * 0.3989422804014327
    return normal_cdf + values * density


def channel_mix(blocks, spectrum):
    block_re = blocks[:, :, 0]
    block_im = blocks[:, :, 1]
    spec_re = spectrum[..., 0]
    spec_im = spectrum[..., 1]
    form = "baoc,czba->ozba"
    out_re = jnp.einsum(form, block_re, spec_re, precision=precise) - jnp.einsum(
        form, block_im, spec_im, precision=precise
    )
    out_im = jnp.einsum(form, block_re, spec_im, precision=precise) + jnp.einsum(
        form, block_im, spec_re, precision=precise
    )
    return jnp.stack([out_re, out_im], -1)


def channel_adjoint(blocks, spectrum):
    block_re = blocks[:, :, 0]
    block_im = blocks[:, :, 1]
    grad_re = spectrum[..., 0]
    grad_im = spectrum[..., 1]
    form = "baoc,ozba->czba"
    out_re = jnp.einsum(form, block_re, grad_re, precision=precise) + jnp.einsum(
        form, block_im, grad_im, precision=precise
    )
    out_im = jnp.einsum(form, block_re, grad_im, precision=precise) - jnp.einsum(
        form, block_im, grad_re, precision=precise
    )
    return jnp.stack([out_re, out_im], -1)


def block_gradient(spectrum_grad, spectrum):
    grad_re = spectrum_grad[..., 0]
    grad_im = spectrum_grad[..., 1]
    spec_re = spectrum[..., 0]
    spec_im = spectrum[..., 1]
    form = "ozba,czba->aboc"
    out_re = jnp.einsum(form, grad_re, spec_re, precision=precise) + jnp.einsum(
        form, grad_im, spec_im, precision=precise
    )
    out_im = jnp.einsum(form, grad_im, spec_re, precision=precise) - jnp.einsum(
        form, grad_re, spec_im, precision=precise
    )
    return jnp.stack([out_re, out_im], 2)


def invert_rows(spectrum, cos_rows, sin_rows):
    spec_re = spectrum[..., 0]
    spec_im = spectrum[..., 1]
    form = "czma,xa->czmx"
    back_re = jnp.einsum(form, spec_re, cos_rows, precision=precise) - jnp.einsum(
        form, spec_im, sin_rows, precision=precise
    )
    back_im = jnp.einsum(form, spec_re, sin_rows, precision=precise) + jnp.einsum(
        form, spec_im, cos_rows, precision=precise
    )
    joined = jnp.stack([back_re, back_im], 3)
    return joined.reshape(joined.shape[0], joined.shape[1], 2 * joined.shape[2], joined.shape[4])


def on_device(
    field_in,
    cotangent,
    spectrum_saved,
    weight_store,
    block_slot,
    kx_modes,
    ky_modes,
    pointwise,
    bias_vector,
):
    channels, planes, rows_x, width_y = field_in.shape
    full_x = rows_x * lax.axis_size("px")
    modes_y = ky_modes.shape[0]
    local_y = modes_y // lax.axis_size("px")
    capacity = weight_store.shape[0]
    factor = 1.0 / math.sqrt(full_x * width_y)
    cos_y, sin_y = phase_table(width_y, ky_modes)
    table_y = jnp.stack([cos_y, -sin_y], 2).reshape(width_y, 2 * modes_y)
    cos_x, sin_x = phase_table(full_x, kx_modes)
    count_py = lax.axis_size("py")
    wide = 2 * channels
    pieces_out = jnp.transpose(weight_store, (2, 0, 1, 3)).reshape(channels, capacity * wide)
    slots_out = jnp.broadcast_to(
        block_slot.astype(jnp.float32).reshape(1, local_y), (count_py, local_y)
    )
    arrived = lax.all_to_all(
        jnp.concatenate([pieces_out, slots_out], 1), "py", split_axis=0, concat_axis=0, tiled=True
    )
    pieces_row = arrived[:, : capacity * wide].reshape(count_py * capacity, wide)
    slots_flat = arrived[:, capacity * wide :].reshape(-1).astype(jnp.int32)
    select = (
        slots_flat[:, None] == lax.iota(jnp.int32, count_py * capacity)[None, :]
    ).astype(jnp.float32)
    chosen = jnp.dot(select, pieces_row, precision=precise).reshape(count_py, local_y * wide)
    rows_mine = lax.all_to_all(chosen, "py", split_axis=0, concat_axis=0, tiled=True)

    def inverse_planes(spectrum):
        joined = invert_rows(spectrum, cos_x, sin_x)
        returned = lax.all_to_all(joined, "px", split_axis=3, concat_axis=2, tiled=True)
        return factor * jnp.einsum("czkx,yk->czxy", returned, table_y, precision=precise)

    weight_full = pointwise.astype(jnp.float32)
    blocks = jnp.transpose(
        rows_mine.reshape(channels, local_y, 1, 2, channels), (1, 2, 3, 0, 4)
    )
    mixed = channel_mix(blocks, spectrum_saved)

    def from_modes(spectrum):
        return lax.all_to_all(spectrum, "py", split_axis=1, concat_axis=3, tiled=True)

    spectral = inverse_planes(from_modes(mixed))
    mapped = jnp.einsum("oc,czxy->ozxy", pointwise, field_in, preferred_element_type=jnp.float32)
    grad = cotangent.astype(jnp.float32) * gelu_slope(
        mapped + bias_vector.reshape(channels, 1, 1, 1) + spectral
    )
    partial_value = jnp.einsum("czxy,yk->czkx", grad, table_y, precision=precise)
    moved = lax.all_to_all(partial_value, "px", split_axis=2, concat_axis=3, tiled=True)
    pieces = moved.reshape(channels, planes, local_y, 2, full_x)
    part_re = pieces[:, :, :, 0]
    part_im = pieces[:, :, :, 1]
    form = "czmx,xk->czmk"
    real_part = jnp.einsum(form, part_re, cos_x, precision=precise) + jnp.einsum(
        form, part_im, sin_x, precision=precise
    )
    imag_part = jnp.einsum(form, part_im, cos_x, precision=precise) - jnp.einsum(
        form, part_re, sin_x, precision=precise
    )
    spectrum_grad = lax.all_to_all(
        factor * jnp.stack([real_part, imag_part], -1),
        "py",
        split_axis=3,
        concat_axis=1,
        tiled=True,
    )
    input_spectrum = channel_adjoint(blocks, spectrum_grad)
    local_grad = block_gradient(spectrum_grad, spectrum_saved)
    field_grad = jnp.einsum("oc,ozxy->czxy", weight_full, grad, precision=precise) + inverse_planes(
        from_modes(input_spectrum)
    )
    grads_out = jnp.transpose(local_grad[0], (2, 0, 1, 3)).reshape(channels, local_y * wide)
    grads_row = lax.all_to_all(grads_out, "py", split_axis=0, concat_axis=0, tiled=True)
    placed = jnp.dot(
        select.T, grads_row.reshape(count_py * local_y, wide), precision=precise
    ).reshape(count_py, capacity * wide)
    store_flat = lax.all_to_all(placed, "py", split_axis=0, concat_axis=0, tiled=True)
    store_grad = jnp.transpose(
        store_flat.reshape(channels, capacity, 2, channels), (1, 2, 0, 3)
    )
    return (field_grad, store_grad)


def solution(mesh):
    placed = (
        P(None, "py", "px", None),
        P(None, "py", "px", None),
        P(None, None, "px", "py", None),
        P(("px", "py"), None, None, None),
        P("py", "px"),
        P(),
        P(),
        P(),
        P(),
    )
    return jax.shard_map(
        on_device,
        mesh=mesh,
        in_specs=placed,
        out_specs=(P(None, "py", "px", None), P(("px", "py"), None, None, None)),
        check_vma=False,
    )
```

```python
import functools
import math

import jax
import jax.numpy as jnp
from jax import lax
from jax.experimental import pallas as pl
from jax.experimental.pallas import tpu as pltpu
from jax.sharding import PartitionSpec as P

MESH = pl.DeviceIdType.MESH
HIGH = lax.Precision.HIGH
EXACT = lax.Precision.HIGHEST
NN = (((1,), (0,)), ((), ()))
NT = (((1,), (1,)), ((), ()))
TN = (((0,), (0,)), ((), ()))


def dot(a, b, dims, precision=HIGH):
    return lax.dot_general(
        a, b, dims, precision=precision, preferred_element_type=jnp.float32
    )


def gelu_slope(values):
    normal_cdf = 0.5 * (1.0 + lax.erf(values * 0.7071067811865476))
    density = jnp.exp(-0.5 * values * values) * 0.3989422804014327
    return normal_cdf + values * density


def iota(shape, axis):
    return lax.broadcasted_iota(jnp.int32, shape, axis)


def spread_map(pointwise, group, dims):
    channels = pointwise.shape[0]
    size = channels * group
    left = (iota((size, channels), 0) // group == iota((size, channels), 1)).astype(jnp.bfloat16)
    right = (iota((channels, size), 1) // group == iota((channels, size), 0)).astype(jnp.bfloat16)
    half = lax.dot_general(left, pointwise, dims, preferred_element_type=jnp.float32)
    full = jnp.dot(half.astype(jnp.bfloat16), right, preferred_element_type=jnp.float32)
    same = (iota((size, size), 0) & (group - 1)) == (iota((size, size), 1) & (group - 1))
    return jnp.where(same, full, 0.0).astype(jnp.bfloat16)


def turned(values, imag):
    return jnp.where(imag, pltpu.roll(values, 32, 1), -pltpu.roll(values, 96, 1))


def kernel(
    n_px,
    n_py,
    field_hbm,
    cot_hbm,
    saved_ref,
    store_ref,
    slots_ref,
    table_x_ref,
    table_y_ref,
    pointwise_ref,
    bias_ref,
    out_hbm,
    store_out_ref,
    field_ref,
    cot_ref,
    pre_ref,
    grad_ref,
    rows_ref,
    back_ref,
    piece_out,
    piece_in,
    chosen_out,
    chosen_in,
    mixed_out,
    mixed_in,
    plane_out,
    plane_in,
    part_out,
    part_in,
    whole_out,
    whole_in,
    adj_out,
    adj_in,
    last_out,
    last_in,
    block_out,
    block_in,
    slot_out,
    slot_in,
    send_sem,
    recv_sem,
    local_sem,
):
    mine_x = lax.axis_index("px")
    mine_y = lax.axis_index("py")
    channels = 32
    groups = channels // 4

    def send(phase, src, dst, axis, whole=False):
        n, me = (n_px, mine_x) if axis == "px" else (n_py, mine_y)

        def one(step, carry):
            peer = lax.rem(me + step, n)
            pltpu.make_async_remote_copy(
                src_ref=src if whole else src.at[peer],
                dst_ref=dst.at[me],
                send_sem=send_sem.at[phase],
                recv_sem=recv_sem.at[phase],
                device_id={axis: peer},
                device_id_type=MESH,
            ).start()
            return carry

        lax.fori_loop(1, n, one, 0)
        dst[me] = src[...] if whole else src[me]

    def bulk(phase, dst, axis):
        n, me = (n_px, mine_x) if axis == "px" else (n_py, mine_y)
        span = dst.at[pl.ds(0, n - 1)]
        return pltpu.make_async_remote_copy(
            src_ref=span,
            dst_ref=span,
            send_sem=send_sem.at[phase],
            recv_sem=recv_sem.at[phase],
            device_id={axis: lax.rem(me + 1, n)},
            device_id_type=MESH,
        )

    field_copy = pltpu.make_async_copy(field_hbm, field_ref, local_sem.at[0])
    cot_copy = pltpu.make_async_copy(cot_hbm, cot_ref, local_sem.at[1])
    field_copy.start()
    cot_copy.start()

    barrier = pltpu.get_barrier_semaphore()

    def greet(axis):
        n, me = (n_px, mine_x) if axis == "px" else (n_py, mine_y)

        def one(step, carry):
            pl.semaphore_signal(
                barrier, inc=1, device_id={axis: lax.rem(me + step, n)}, device_id_type=MESH
            )
            return carry

        lax.fori_loop(1, n, one, 0)

    greet("py")
    greet("px")

    wide = jnp.concatenate([store_ref[k] for k in range(8)], axis=1)
    piece_out[:, 0, 0:256] = wide
    piece_out[:, 0, 256:384] = jnp.broadcast_to(slots_ref[...], (n_py, 128))
    pl.semaphore_wait(barrier, n_px + n_py - 2)
    send(0, piece_out, piece_in, "py")

    pointwise = pointwise_ref[...]
    forward_map = spread_map(pointwise, 16, NN)
    backward_map = spread_map(pointwise, 8, NT)
    field_copy.wait()
    for part in range(2):
        cut = pl.ds(16 * part, 16)
        block = field_ref[:, cut, :].reshape(16 * channels, 512)
        mapped = jnp.dot(forward_map, block, preferred_element_type=jnp.float32)
        pre_ref[:, cut, :] = mapped.reshape(channels, 16, 512)

    lane = iota((1, 128), 1)
    imag = (lane & 32) != 0
    first = lane < 64
    slot_of_lane = ((lane & 31) * 4 + (lane >> 5)).astype(jnp.float32)

    bulk(0, piece_in, "py").wait_recv()
    pieces = jnp.concatenate([piece_in[:, 0, 64 * s : 64 * s + 64] for s in range(4)], axis=0)
    slots = piece_in[:, 0, 256:384]
    selects = [
        jnp.where(slots[:, b : b + 1] == slot_of_lane, 1.0, 0.0).astype(jnp.float32)
        for b in range(2)
    ]
    chosen_out[:, 0, :] = jnp.concatenate(
        [dot(select, pieces, NN, EXACT) for select in selects], axis=1
    )
    send(1, chosen_out, chosen_in, "py")

    saved = saved_ref[...]
    table_x = table_x_ref[...]
    table_y = table_y_ref[...]

    bulk(1, chosen_in, "py").wait_recv()
    weights = chosen_in[:, 0, :]
    signed = jnp.where(imag, -weights, weights)
    swapped = jnp.where(imag, pltpu.roll(weights, 32, 1), pltpu.roll(weights, 96, 1))
    mix = jnp.concatenate(
        [
            jnp.where(first, signed, 0.0),
            jnp.where(first, swapped, 0.0),
            jnp.where(first, 0.0, signed),
            jnp.where(first, 0.0, swapped),
        ],
        axis=0,
    )
    mixed_out[:, 0, :] = dot(saved, mix, NT)
    send(2, mixed_out, mixed_in, "py")

    bulk(2, mixed_in, "py").wait_recv()
    plane_out[...] = mixed_in[:, 0, :]
    send(3, plane_out, plane_in, "px", whole=True)

    def to_rows(planes):
        def one(p, carry):
            plane = planes[p]
            both = jnp.concatenate([plane, turned(plane, imag)], axis=0)
            rows_ref[pl.ds(pl.multiple_of(p * 128, 128), 128), :] = dot(both, table_x, TN)
            return carry

        lax.fori_loop(0, n_px, one, 0)

    lane_group = lane >> 5

    def row_block(i):
        picked = rows_ref[pl.ds(4 * i, 64, stride=32), :]
        for g in range(1, 4):
            picked = jnp.where(
                lane_group == g, rows_ref[pl.ds(4 * i + g, 64, stride=32), :], picked
            )
        return dot(picked, table_y, TN)

    cot_copy.wait()
    bulk(3, plane_in, "px").wait_recv()
    to_rows(plane_in)

    def grad_block(i, carry):
        spectral = row_block(i)
        parts = []
        for g in range(4):
            o = 4 * i + g
            pre = pre_ref[o] + bias_ref[o] + spectral[32 * g : 32 * g + 32]
            grad = cot_ref[o].astype(jnp.float32) * gelu_slope(pre)
            grad_ref[o] = grad
            parts.append(grad)
        freq = dot(table_y, jnp.concatenate(parts, axis=0), NT)
        for g in range(4):
            back_ref[pl.ds(4 * i + g, 64, stride=32), :] = freq
        return carry

    lax.fori_loop(0, groups, grad_block, 0)

    own_group = (iota((128, 128), 0) & 3) == (iota((128, 128), 1) >> 5)

    def part_block(p, carry):
        rows = back_ref[pl.ds(pl.multiple_of(p * 128, 128), 128), :]
        both = dot(table_x, jnp.where(own_group, rows, 0.0), NT)
        part_out[p] = both[0:32] - turned(both[32:64], imag)
        return carry

    lax.fori_loop(0, n_px, part_block, 0)
    send(4, part_out, part_in, "px")

    for part in range(4):
        cut = pl.ds(8 * part, 8)
        block = grad_ref[:, cut, :].reshape(8 * channels, 512)
        upper = block.astype(jnp.bfloat16)
        lower = (block - upper.astype(jnp.float32)).astype(jnp.bfloat16)
        base = jnp.dot(backward_map, upper, preferred_element_type=jnp.float32) + jnp.dot(
            backward_map, lower, preferred_element_type=jnp.float32
        )
        pre_ref[:, cut, :] = base.reshape(channels, 8, 512)

    bulk(4, part_in, "px").wait_recv()
    total = part_in[0]
    for p in range(1, n_px):
        total = total + part_in[p]
    whole_out[:, 0, :] = total
    send(5, whole_out, whole_in, "py")

    bulk(5, whole_in, "py").wait_recv()
    spectrum_grad = whole_in[:, 0, :]
    adj_out[:, 0, :] = dot(spectrum_grad, mix, NN)
    send(6, adj_out, adj_in, "py")

    cross = dot(spectrum_grad, saved, TN)
    blocks = None
    for b in range(2):
        re = cross[64 * b : 64 * b + 32]
        im = cross[64 * b + 32 : 64 * b + 64]
        value = jnp.where(
            imag, im_shift(im, 32) - re, re + im_shift(im, 96)
        )
        blocks = value if b == 0 else jnp.where(first, blocks, value)
    block_out[:, 0, :] = blocks
    send(7, block_out, block_in, "py")

    bulk(6, adj_in, "py").wait_recv()
    last_out[...] = adj_in[:, 0, :]
    send(8, last_out, last_in, "px", whole=True)

    bulk(7, block_in, "py").wait_recv()
    received = block_in[:, 0, :]
    placed = dot(selects[0], received[:, 0:64], TN, EXACT) + dot(
        selects[1], received[:, 64:128], TN, EXACT
    )
    slot_out[:, 0, :] = jnp.concatenate([placed[32 * s : 32 * s + 32] for s in range(4)], axis=1)
    send(9, slot_out, slot_in, "py")

    bulk(8, last_in, "px").wait_recv()
    to_rows(last_in)

    def out_copy(i):
        cut = pl.ds(4 * i, 4)
        return pltpu.make_async_copy(pre_ref.at[cut], out_hbm.at[cut], local_sem.at[2])

    def out_block(i, carry):
        spectral = row_block(i)
        for g in range(4):
            o = 4 * i + g
            pre_ref[o] = pre_ref[o] + spectral[32 * g : 32 * g + 32]
        return carry

    lax.fori_loop(0, groups, out_block, 0)
    final = pltpu.make_async_copy(pre_ref, out_hbm, local_sem.at[2])
    final.start()

    bulk(9, slot_in, "py").wait_recv()
    for k in range(8):
        store_out_ref[k] = slot_in[:, 0, 32 * k : 32 * k + 32]
    final.wait()
    for phase, dst, axis in (
        (0, piece_in, "py"),
        (1, chosen_in, "py"),
        (2, mixed_in, "py"),
        (3, plane_in, "px"),
        (4, part_in, "px"),
        (5, whole_in, "py"),
        (6, adj_in, "py"),
        (7, block_in, "py"),
        (8, last_in, "px"),
        (9, slot_in, "py"),
    ):
        bulk(phase, dst, axis).wait_send()


def im_shift(values, amount):
    return pltpu.roll(values, amount, 1)


def on_device(
    n_px,
    n_py,
    field_in,
    cotangent,
    spectrum_saved,
    weight_store,
    block_slot,
    kx_modes,
    ky_modes,
    pointwise,
    bias_vector,
):
    channels, _, rows_x, width_y = field_in.shape
    full_x = rows_x * n_px
    factor = 1.0 / math.sqrt(full_x * width_y)
    points_y = lax.iota(jnp.int32, width_y)
    angle_y = (points_y[None, :] * ky_modes[:, None] % width_y).astype(jnp.float32) * (
        2.0 * math.pi / width_y
    )
    table_y = jnp.stack([jnp.cos(angle_y), -jnp.sin(angle_y)], 1).reshape(-1, width_y)
    points_x = lax.axis_index("px") * rows_x + (lax.iota(jnp.int32, 4 * rows_x) % rows_x)
    angle_x = (points_x[None, :] * kx_modes[:, None] % full_x).astype(jnp.float32) * (
        2.0 * math.pi / full_x
    )
    table_x = factor * jnp.concatenate([jnp.cos(angle_x), jnp.sin(angle_x)], 0)
    saved = jnp.transpose(spectrum_saved[:, :, :, 0, :], (1, 2, 3, 0)).reshape(n_py, 4 * channels)
    slots = jnp.pad(block_slot.astype(jnp.float32), ((0, 0), (0, 126)))
    vmem = pl.BlockSpec(memory_space=pltpu.VMEM)
    hbm = pl.BlockSpec(memory_space=pl.ANY)
    f32 = jnp.float32
    row = pltpu.VMEM((n_py, 1, 128), f32)
    tile = pltpu.VMEM((32, 128), f32)
    tiles = pltpu.VMEM((n_px, 32, 128), f32)
    field_grad, store_grad = pl.pallas_call(
        functools.partial(kernel, n_px, n_py),
        out_shape=(
            jax.ShapeDtypeStruct((channels, rows_x, width_y), f32),
            jax.ShapeDtypeStruct((8, channels, channels), f32),
        ),
        in_specs=[hbm, hbm, vmem, vmem, vmem, vmem, vmem, vmem]
        + [pl.BlockSpec(memory_space=pltpu.SMEM)],
        out_specs=(hbm, vmem),
        scratch_shapes=[
            pltpu.VMEM((channels, rows_x, width_y), jnp.bfloat16),
            pltpu.VMEM((channels, rows_x, width_y), jnp.bfloat16),
            pltpu.VMEM((channels, rows_x, width_y), f32),
            pltpu.VMEM((channels, rows_x, width_y), f32),
            pltpu.VMEM((n_px * 128, 128), f32),
            pltpu.VMEM((n_px * 128, 128), f32),
            pltpu.VMEM((n_py, 1, 384), f32),
            pltpu.VMEM((n_py, 1, 384), f32),
            row,
            row,
            row,
            row,
            tile,
            tiles,
            tiles,
            tiles,
            row,
            row,
            row,
            row,
            tile,
            tiles,
            row,
            row,
            pltpu.VMEM((n_py, 1, 256), f32),
            pltpu.VMEM((n_py, 1, 256), f32),
            pltpu.SemaphoreType.DMA((10,)),
            pltpu.SemaphoreType.DMA((10,)),
            pltpu.SemaphoreType.DMA((3,)),
        ],
        compiler_params=pltpu.CompilerParams(
            collective_id=0, has_side_effects=True, vmem_limit_bytes=48 << 20
        ),
    )(
        field_in.reshape(channels, rows_x, width_y),
        cotangent.reshape(channels, rows_x, width_y),
        saved,
        weight_store.reshape(8, channels, channels),
        slots,
        table_x,
        table_y,
        pointwise,
        bias_vector,
    )
    return (
        field_grad.reshape(field_in.shape),
        store_grad.reshape(weight_store.shape),
    )


def solution(mesh):
    placed = (
        P(None, "py", "px", None),
        P(None, "py", "px", None),
        P(None, None, "px", "py", None),
        P(("px", "py"), None, None, None),
        P("py", "px"),
        P(),
        P(),
        P(),
        P(),
    )
    return jax.shard_map(
        functools.partial(on_device, mesh.shape["px"], mesh.shape["py"]),
        mesh=mesh,
        in_specs=placed,
        out_specs=(P(None, "py", "px", None), P(("px", "py"), None, None, None)),
        check_vma=False,
    )
```

```python
import functools
import math

import jax
import jax.numpy as jnp
from jax import lax
from jax.experimental import pallas as pl
from jax.experimental.pallas import tpu as pltpu
from jax.sharding import PartitionSpec as P

MESH = pl.DeviceIdType.MESH
HIGH = lax.Precision.HIGH
EXACT = lax.Precision.HIGHEST
NN = (((1,), (0,)), ((), ()))
NT = (((1,), (1,)), ((), ()))
TN = (((0,), (0,)), ((), ()))
STEPS = (1, 7, 2, 6, 3, 5, 4)
BATCHES = ((1, 7, 2, 6), (3, 5, 4))


def dot(a, b, dims, precision=HIGH):
    return lax.dot_general(
        a, b, dims, precision=precision, preferred_element_type=jnp.float32
    )


def gelu_slope(values):
    normal_cdf = 0.5 * (1.0 + lax.erf(values * 0.7071067811865476))
    density = jnp.exp(-0.5 * values * values) * 0.3989422804014327
    return normal_cdf + values * density


def iota(shape, axis):
    return lax.broadcasted_iota(jnp.int32, shape, axis)


def spread_map(pointwise, group, dims):
    channels = pointwise.shape[0]
    size = channels * group
    left = (iota((size, channels), 0) // group == iota((size, channels), 1)).astype(jnp.bfloat16)
    right = (iota((channels, size), 1) // group == iota((channels, size), 0)).astype(jnp.bfloat16)
    half = lax.dot_general(left, pointwise, dims, preferred_element_type=jnp.float32)
    full = jnp.dot(half.astype(jnp.bfloat16), right, preferred_element_type=jnp.float32)
    same = (iota((size, size), 0) & (group - 1)) == (iota((size, size), 1) & (group - 1))
    return jnp.where(same, full, 0.0).astype(jnp.bfloat16)


def column(row_ref, size, repeat):
    count = row_ref.shape[1]
    same = iota((size, count), 0) // repeat == iota((size, count), 1)
    row = row_ref[...].astype(jnp.float32)
    return jnp.sum(jnp.where(same, row, 0.0), axis=1, keepdims=True).astype(jnp.int32)


def angle(points, length):
    return (points & (length - 1)).astype(jnp.float32) * (2.0 * math.pi / length)


def turned(values, imag):
    return jnp.where(imag, pltpu.roll(values, 32, 1), -pltpu.roll(values, 96, 1))


def kernel(
    n_px,
    n_py,
    field_hbm,
    cot_hbm,
    saved_hbm,
    store_hbm,
    slots_hbm,
    kx_hbm,
    ky_hbm,
    pointwise_hbm,
    bias_hbm,
    out_hbm,
    store_out_hbm,
    field_ref,
    cot_ref,
    saved_ref,
    store_ref,
    slots_ref,
    kx_ref,
    ky_ref,
    pointwise_ref,
    bias_ref,
    table_y_ref,
    store_out_ref,
    pre_ref,
    grad_ref,
    rows_ref,
    back_ref,
    piece_out,
    piece_in,
    chosen_out,
    chosen_in,
    mixed_out,
    mixed_in,
    plane_out,
    plane_in,
    part_out,
    part_in,
    half_in,
    whole_out,
    whole_in,
    adj_out,
    adj_in,
    last_out,
    last_in,
    block_out,
    block_in,
    slot_out,
    slot_in,
    send_sem,
    recv_sem,
    px_sem,
    part_sem,
    local_sem,
):
    mine_x = lax.axis_index("px")
    mine_y = lax.axis_index("py")
    sibling = mine_x + 1 - 2 * lax.rem(mine_x, 2)
    full_x = 32 * n_px
    factor = 1.0 / math.sqrt(full_x * 512)
    channels = 32
    groups = channels // 4

    def send(phase, src, dst, axis, whole=False):
        n, me = (n_px, mine_x) if axis == "px" else (n_py, mine_y)

        def one(step, carry):
            peer = lax.rem(me + step, n)
            pltpu.make_async_remote_copy(
                src_ref=src if whole else src.at[peer],
                dst_ref=dst.at[me],
                send_sem=send_sem.at[phase],
                recv_sem=recv_sem.at[phase],
                device_id={axis: peer},
                device_id_type=MESH,
            ).start()
            return carry

        lax.fori_loop(1, n, one, 0)
        dst[me] = src[...] if whole else src[me]

    def bulk(phase, dst, axis):
        n, me = (n_px, mine_x) if axis == "px" else (n_py, mine_y)
        span = dst.at[pl.ds(0, n - 1)]
        return pltpu.make_async_remote_copy(
            src_ref=span,
            dst_ref=span,
            send_sem=send_sem.at[phase],
            recv_sem=recv_sem.at[phase],
            device_id={axis: lax.rem(me + 1, n)},
            device_id_type=MESH,
        )

    loads = [
        pltpu.make_async_copy(src, dst, local_sem.at[k])
        for k, (src, dst) in enumerate(
            (
                (store_hbm, store_ref),
                (slots_hbm, slots_ref),
                (kx_hbm, kx_ref),
                (ky_hbm, ky_ref),
                (pointwise_hbm, pointwise_ref),
                (bias_hbm, bias_ref),
                (saved_hbm, saved_ref),
                (field_hbm, field_ref),
                (cot_hbm, cot_ref),
            )
        )
    ]
    for load in loads:
        load.start()

    barrier = pltpu.get_barrier_semaphore()

    def signal_px(peer):
        pl.semaphore_signal(barrier, inc=1, device_id={"px": peer}, device_id_type=MESH)

    def greet(axis):
        n, me = (n_px, mine_x) if axis == "px" else (n_py, mine_y)

        def one(step, carry):
            pl.semaphore_signal(
                barrier, inc=1, device_id={axis: lax.rem(me + step, n)}, device_id_type=MESH
            )
            return carry

        lax.fori_loop(1, n, one, 0)

    greet("py")
    for step in STEPS:
        signal_px(lax.rem(mine_x + 2 * step, n_px))
    signal_px(sibling)

    loads[0].wait()
    loads[1].wait()
    wide = jnp.concatenate([store_ref[k] for k in range(8)], axis=1)
    piece_out[:, 0, 0:256] = wide
    piece_out[:, 0, 256:384] = jnp.zeros((n_py, 128), jnp.float32)
    piece_out[:, 0, 256:258] = jnp.broadcast_to(slots_ref[...].astype(jnp.float32), (n_py, 2))
    pl.semaphore_wait(barrier, n_py + len(STEPS))
    send(0, piece_out, piece_in, "py")

    for load in loads[2:8]:
        load.wait()
    pointwise = pointwise_ref[...]
    forward_map = spread_map(pointwise, 16, NN)
    backward_map = spread_map(pointwise, 8, NT)
    owner = iota((16 * channels, channels), 0) // 16 == iota((16 * channels, channels), 1)
    bias = jnp.sum(jnp.where(owner, bias_ref[...], 0.0), axis=1, keepdims=True)
    for part in range(2):
        cut = pl.ds(16 * part, 16)
        block = field_ref[:, cut, :].reshape(16 * channels, 512)
        mapped = jnp.dot(forward_map, block, preferred_element_type=jnp.float32) + bias
        pre_ref[:, cut, :] = mapped.reshape(channels, 16, 512)

    lane = iota((1, 128), 1)
    imag = (lane & 32) != 0
    first = lane < 64
    slot_of_lane = ((lane & 31) * 4 + (lane >> 5)).astype(jnp.float32)

    bulk(0, piece_in, "py").wait_recv()
    pieces = jnp.concatenate([piece_in[:, 0, 64 * s : 64 * s + 64] for s in range(4)], axis=0)
    slots = piece_in[:, 0, 256:384]
    selects = [
        jnp.where(slots[:, b : b + 1] == slot_of_lane, 1.0, 0.0).astype(jnp.float32)
        for b in range(2)
    ]
    chosen_out[:, 0, :] = jnp.concatenate(
        [dot(select, pieces, NN, EXACT) for select in selects], axis=1
    )
    send(1, chosen_out, chosen_in, "py")

    saved = jnp.concatenate(
        [saved_ref[:, b, r, :] for b in range(2) for r in range(2)], axis=0
    ).T
    kx = column(kx_ref, 32, 1)
    angle_x = angle((mine_x * 32 + (iota((32, 128), 1) & 31)) * kx, full_x)
    table_x = jnp.concatenate([jnp.cos(angle_x), jnp.sin(angle_x)], axis=0) * factor
    ky = column(ky_ref, 64, 2)
    angle_y = angle(iota((64, 512), 1) * ky, 512)
    even = (iota((64, 512), 0) & 1) == 0
    table_y_ref[...] = jnp.where(even, jnp.cos(angle_y), -jnp.sin(angle_y))
    table_y = table_y_ref[...]

    bulk(1, chosen_in, "py").wait_recv()
    weights = chosen_in[:, 0, :]
    signed = jnp.where(imag, -weights, weights)
    swapped = jnp.where(imag, pltpu.roll(weights, 32, 1), pltpu.roll(weights, 96, 1))
    mix = jnp.concatenate(
        [
            jnp.where(first, signed, 0.0),
            jnp.where(first, swapped, 0.0),
            jnp.where(first, 0.0, signed),
            jnp.where(first, 0.0, swapped),
        ],
        axis=0,
    )
    mixed_out[:, 0, :] = dot(saved, mix, NT)
    send(2, mixed_out, mixed_in, "py")

    def px_copy(k, src, dst, source, peer):
        return pltpu.make_async_remote_copy(
            src_ref=src,
            dst_ref=dst,
            send_sem=send_sem.at[(3, 4, 8)[k]],
            recv_sem=px_sem.at[k, source],
            device_id={"px": peer},
            device_id_type=MESH,
        )

    def to_rows(planes, sources):
        both = jnp.concatenate(
            [
                jnp.concatenate([planes[p], turned(planes[p], imag)], axis=0)
                for p in sources
            ],
            axis=1,
        )
        rows = dot(both, table_x, TN)
        for n, p in enumerate(sources):
            rows_ref[pl.ds(pl.multiple_of(p * 128, 128), 128), :] = rows[
                128 * n : 128 * n + 128
            ]

    def scatter_plane(k, src, dst):
        px_copy(k, src, dst.at[mine_x], mine_x, sibling).start()
        for step in STEPS:
            peer = lax.rem(mine_x + 2 * step, n_px)
            px_copy(k, src, dst.at[mine_x], mine_x, peer).start()
        dst[mine_x] = src[...]

    def collect_planes(k, dst):
        def arrived(p):
            px_copy(k, dst.at[p], dst.at[p], p, sibling).wait_recv()

        arrived(sibling)
        to_rows(dst, [mine_x, sibling])
        for batch in BATCHES:
            sources = [lax.rem(mine_x + n_px - 2 * step, n_px) for step in batch]
            for p in sources:
                arrived(p)
                px_copy(k, dst.at[p], dst.at[p], p, sibling).start()
            to_rows(dst, sources)
        for batch in BATCHES:
            sources = [lax.rem(sibling + n_px - 2 * step, n_px) for step in batch]
            for p in sources:
                arrived(p)
            to_rows(dst, sources)

    bulk(2, mixed_in, "py").wait_recv()
    plane_out[...] = mixed_in[:, 0, :]
    scatter_plane(0, plane_out, plane_in)

    lane_group = lane >> 5

    def row_block(i):
        picked = rows_ref[pl.ds(4 * i, 64, stride=32), :]
        for g in range(1, 4):
            picked = jnp.where(
                lane_group == g, rows_ref[pl.ds(4 * i + g, 64, stride=32), :], picked
            )
        return dot(picked, table_y, TN)

    loads[8].wait()
    collect_planes(0, plane_in)

    def grad_block(i, carry):
        spectral = row_block(i)
        parts = []
        for g in range(4):
            o = 4 * i + g
            pre = pre_ref[o] + spectral[32 * g : 32 * g + 32]
            grad = cot_ref[o].astype(jnp.float32) * gelu_slope(pre)
            grad_ref[o] = grad
            parts.append(grad)
        freq = dot(table_y, jnp.concatenate(parts, axis=0), NT)
        for g in range(4):
            back_ref[pl.ds(4 * i + g, 64, stride=32), :] = freq
        return carry

    lax.fori_loop(0, groups, grad_block, 0)

    own_group = (iota((128, 128), 0) & 3) == (iota((128, 128), 1) >> 5)

    def part_tiles(targets):
        rows = jnp.concatenate(
            [
                jnp.where(
                    own_group, back_ref[pl.ds(pl.multiple_of(p * 128, 128), 128), :], 0.0
                )
                for p in targets
            ],
            axis=0,
        )
        both = dot(table_x, rows, NT)
        tiles = [both[:, 128 * n : 128 * n + 128] for n in range(len(targets))]
        return [tile[0:32] - turned(tile[32:64], imag) for tile in tiles]

    for batch in (STEPS[0:4], STEPS[4:] + (0,)):
        targets = [lax.rem(sibling + 2 * step, n_px) for step in batch]
        for p, tile in zip(targets, part_tiles(targets)):
            part_out[p] = tile
            px_copy(1, part_out.at[p], half_in.at[p], p, sibling).start()
    total = None
    for batch in (STEPS[0:4], STEPS[4:] + (0,)):
        targets = [lax.rem(mine_x + 2 * step, n_px) for step in batch]
        for step, p, tile in zip(batch, targets, part_tiles(targets)):
            px_copy(1, half_in.at[p], half_in.at[p], p, sibling).wait_recv()
            tile = tile + half_in[p]
            if step == 0:
                total = tile
            else:
                part_out[p] = tile
                pltpu.make_async_remote_copy(
                    src_ref=part_out.at[p],
                    dst_ref=part_in.at[mine_x],
                    send_sem=send_sem.at[4],
                    recv_sem=part_sem.at[mine_x],
                    device_id={"px": p},
                    device_id_type=MESH,
                ).start()

    for part in range(4):
        cut = pl.ds(8 * part, 8)
        block = grad_ref[:, cut, :].reshape(8 * channels, 512)
        upper = block.astype(jnp.bfloat16)
        lower = (block - upper.astype(jnp.float32)).astype(jnp.bfloat16)
        base = jnp.dot(backward_map, upper, preferred_element_type=jnp.float32) + jnp.dot(
            backward_map, lower, preferred_element_type=jnp.float32
        )
        pre_ref[:, cut, :] = base.reshape(channels, 8, 512)

    for step in STEPS:
        p = lax.rem(mine_x + n_px - 2 * step, n_px)
        pltpu.make_async_remote_copy(
            src_ref=part_in.at[p],
            dst_ref=part_in.at[p],
            send_sem=send_sem.at[4],
            recv_sem=part_sem.at[p],
            device_id={"px": sibling},
            device_id_type=MESH,
        ).wait_recv()
        total = total + part_in[p]
    whole_out[:, 0, :] = total
    send(5, whole_out, whole_in, "py")

    bulk(5, whole_in, "py").wait_recv()
    spectrum_grad = whole_in[:, 0, :]
    adj_out[:, 0, :] = dot(spectrum_grad, mix, NN)
    send(6, adj_out, adj_in, "py")

    cross = dot(spectrum_grad, saved, TN)
    blocks = None
    for b in range(2):
        re = cross[64 * b : 64 * b + 32]
        im = cross[64 * b + 32 : 64 * b + 64]
        value = jnp.where(
            imag, im_shift(im, 32) - re, re + im_shift(im, 96)
        )
        blocks = value if b == 0 else jnp.where(first, blocks, value)
    block_out[:, 0, :] = blocks
    send(7, block_out, block_in, "py")

    bulk(6, adj_in, "py").wait_recv()
    last_out[...] = adj_in[:, 0, :]
    scatter_plane(2, last_out, last_in)

    bulk(7, block_in, "py").wait_recv()
    received = block_in[:, 0, :]
    placed = dot(selects[0], received[:, 0:64], TN, EXACT) + dot(
        selects[1], received[:, 64:128], TN, EXACT
    )
    slot_out[:, 0, :] = jnp.concatenate([placed[32 * s : 32 * s + 32] for s in range(4)], axis=1)
    send(9, slot_out, slot_in, "py")

    collect_planes(2, last_in)

    def out_block(i, carry):
        spectral = row_block(i)
        for g in range(4):
            o = 4 * i + g
            pre_ref[o] = pre_ref[o] + spectral[32 * g : 32 * g + 32]
        cut = pl.ds(4 * i, 4)
        pltpu.make_async_copy(pre_ref.at[cut], out_hbm.at[cut], local_sem.at[9]).start()
        return carry

    lax.fori_loop(0, groups, out_block, 0)
    final = pltpu.make_async_copy(pre_ref, out_hbm, local_sem.at[9])

    bulk(9, slot_in, "py").wait_recv()
    for k in range(8):
        store_out_ref[k] = slot_in[:, 0, 32 * k : 32 * k + 32]
    last = pltpu.make_async_copy(store_out_ref, store_out_hbm, local_sem.at[10])
    last.start()
    final.wait()
    last.wait()
    for phase, dst, axis in (
        (0, piece_in, "py"),
        (1, chosen_in, "py"),
        (2, mixed_in, "py"),
        (3, plane_in, "px"),
        (4, part_in, "px"),
        (5, whole_in, "py"),
        (6, adj_in, "py"),
        (7, block_in, "py"),
        (8, last_in, "px"),
        (9, slot_in, "py"),
    ):
        bulk(phase, dst, axis).wait_send()


def im_shift(values, amount):
    return pltpu.roll(values, amount, 1)


def on_device(
    n_px,
    n_py,
    field_in,
    cotangent,
    spectrum_saved,
    weight_store,
    block_slot,
    kx_modes,
    ky_modes,
    pointwise,
    bias_vector,
):
    channels, _, rows_x, width_y = field_in.shape
    hbm = pl.BlockSpec(memory_space=pltpu.HBM)
    f32 = jnp.float32
    row = pltpu.VMEM((n_py, 1, 128), f32)
    tile = pltpu.VMEM((32, 128), f32)
    tiles = pltpu.VMEM((n_px, 32, 128), f32)
    field_grad, store_grad = pl.pallas_call(
        functools.partial(kernel, n_px, n_py),
        out_shape=(
            jax.ShapeDtypeStruct((channels, rows_x, width_y), f32),
            jax.ShapeDtypeStruct((8, channels, channels), f32),
        ),
        in_specs=[hbm] * 9,
        out_specs=(hbm, hbm),
        scratch_shapes=[
            pltpu.VMEM((channels, rows_x, width_y), jnp.bfloat16),
            pltpu.VMEM((channels, rows_x, width_y), jnp.bfloat16),
            pltpu.VMEM((channels, 2, 2, n_py), f32),
            pltpu.VMEM((8, channels, channels), f32),
            pltpu.VMEM((1, 2), jnp.int32),
            pltpu.VMEM((1, 32), jnp.int32),
            pltpu.VMEM((1, 32), jnp.int32),
            pltpu.VMEM((channels, channels), jnp.bfloat16),
            pltpu.VMEM((1, channels), f32),
            pltpu.VMEM((64, width_y), f32),
            pltpu.VMEM((8, channels, channels), f32),
            pltpu.VMEM((channels, rows_x, width_y), f32),
            pltpu.VMEM((channels, rows_x, width_y), f32),
            pltpu.VMEM((n_px * 128, 128), f32),
            pltpu.VMEM((n_px * 128, 128), f32),
            pltpu.VMEM((n_py, 1, 384), f32),
            pltpu.VMEM((n_py, 1, 384), f32),
            row,
            row,
            row,
            row,
            tile,
            tiles,
            tiles,
            tiles,
            tiles,
            row,
            row,
            row,
            row,
            tile,
            tiles,
            row,
            row,
            pltpu.VMEM((n_py, 1, 256), f32),
            pltpu.VMEM((n_py, 1, 256), f32),
            pltpu.SemaphoreType.DMA((10,)),
            pltpu.SemaphoreType.DMA((10,)),
            pltpu.SemaphoreType.DMA((3, n_px)),
            pltpu.SemaphoreType.DMA((n_px,)),
            pltpu.SemaphoreType.DMA((11,)),
        ],
        compiler_params=pltpu.CompilerParams(
            collective_id=0, has_side_effects=True, vmem_limit_bytes=63 << 20
        ),
    )(
        field_in.reshape(channels, rows_x, width_y),
        cotangent.reshape(channels, rows_x, width_y),
        jnp.transpose(spectrum_saved[:, :, :, 0, :], (0, 2, 3, 1)),
        weight_store.reshape(8, channels, channels),
        block_slot,
        kx_modes.reshape(1, -1),
        ky_modes.reshape(1, -1),
        pointwise,
        bias_vector.reshape(1, -1),
    )
    return (
        field_grad.reshape(field_in.shape),
        store_grad.reshape(weight_store.shape),
    )


def solution(mesh):
    placed = (
        P(None, "py", "px", None),
        P(None, "py", "px", None),
        P(None, None, "px", "py", None),
        P(("px", "py"), None, None, None),
        P("py", "px"),
        P(),
        P(),
        P(),
        P(),
    )
    return jax.shard_map(
        functools.partial(on_device, mesh.shape["px"], mesh.shape["py"]),
        mesh=mesh,
        in_specs=placed,
        out_specs=(P(None, "py", "px", None), P(("px", "py"), None, None, None)),
        check_vma=False,
    )
```

```python
import functools
import math

import jax
import jax.numpy as jnp
from jax import lax
from jax.experimental import pallas as pl
from jax.experimental.pallas import tpu as pltpu
from jax.sharding import PartitionSpec as P

MESH = pl.DeviceIdType.MESH
HIGH = lax.Precision.HIGH
EXACT = lax.Precision.HIGHEST
NN = (((1,), (0,)), ((), ()))
NT = (((1,), (1,)), ((), ()))
TN = (((0,), (0,)), ((), ()))
STEPS = (1, 7, 2, 6, 3, 5, 4)
BATCHES = ((1, 7, 2, 6), (3, 5, 4))


def dot(a, b, dims, precision=HIGH):
    return lax.dot_general(
        a, b, dims, precision=precision, preferred_element_type=jnp.float32
    )


def gelu_slope(values):
    normal_cdf = 0.5 * (1.0 + lax.erf(values * 0.7071067811865476))
    density = jnp.exp(-0.5 * values * values) * 0.3989422804014327
    return normal_cdf + values * density


def iota(shape, axis):
    return lax.broadcasted_iota(jnp.int32, shape, axis)


def spread_map(pointwise, group, dims):
    channels = pointwise.shape[0]
    size = channels * group
    left = (iota((size, channels), 0) // group == iota((size, channels), 1)).astype(jnp.bfloat16)
    right = (iota((channels, size), 1) // group == iota((channels, size), 0)).astype(jnp.bfloat16)
    half = lax.dot_general(left, pointwise, dims, preferred_element_type=jnp.float32)
    full = jnp.dot(half.astype(jnp.bfloat16), right, preferred_element_type=jnp.float32)
    same = (iota((size, size), 0) & (group - 1)) == (iota((size, size), 1) & (group - 1))
    return jnp.where(same, full, 0.0).astype(jnp.bfloat16)


def column(row_ref, size, repeat):
    count = row_ref.shape[1]
    same = iota((size, count), 0) // repeat == iota((size, count), 1)
    row = row_ref[...].astype(jnp.float32)
    return jnp.sum(jnp.where(same, row, 0.0), axis=1, keepdims=True).astype(jnp.int32)


def angle(points, length):
    return (points & (length - 1)).astype(jnp.float32) * (2.0 * math.pi / length)


def turned(values, imag):
    return jnp.where(imag, pltpu.roll(values, 32, 1), -pltpu.roll(values, 96, 1))


def kernel(
    n_px,
    n_py,
    field_hbm,
    cot_hbm,
    saved_hbm,
    store_hbm,
    slots_hbm,
    kx_hbm,
    ky_hbm,
    pointwise_hbm,
    bias_hbm,
    out_ref,
    store_out_ref,
    field_ref,
    cot_ref,
    saved_ref,
    store_ref,
    slots_ref,
    kx_ref,
    ky_ref,
    pointwise_ref,
    bias_ref,
    table_y_ref,
    pre_ref,
    grad_ref,
    rows_ref,
    back_ref,
    piece_out,
    piece_in,
    chosen_out,
    chosen_in,
    mixed_out,
    mixed_in,
    plane_out,
    plane_in,
    part_out,
    part_in,
    half_in,
    whole_out,
    whole_in,
    wall_out,
    wall_in,
    last_out,
    last_in,
    block_out,
    block_in,
    slot_out,
    slot_in,
    send_sem,
    recv_sem,
    px_sem,
    part_sem,
    local_sem,
):
    mine_x = lax.axis_index("px")
    mine_y = lax.axis_index("py")
    sibling = mine_x + 1 - 2 * lax.rem(mine_x, 2)
    full_x = 32 * n_px
    factor = 1.0 / math.sqrt(full_x * 512)
    channels = 32
    groups = channels // 4

    def send(phase, src, dst, axis, whole=False):
        n, me = (n_px, mine_x) if axis == "px" else (n_py, mine_y)

        def one(step, carry):
            peer = lax.rem(me + step, n)
            pltpu.make_async_remote_copy(
                src_ref=src if whole else src.at[peer],
                dst_ref=dst.at[me],
                send_sem=send_sem.at[phase],
                recv_sem=recv_sem.at[phase],
                device_id={axis: peer},
                device_id_type=MESH,
            ).start()
            return carry

        lax.fori_loop(1, n, one, 0)
        dst[me] = src[...] if whole else src[me]

    def bulk(phase, dst, axis):
        n, me = (n_px, mine_x) if axis == "px" else (n_py, mine_y)
        span = dst.at[pl.ds(0, n - 1)]
        return pltpu.make_async_remote_copy(
            src_ref=span,
            dst_ref=span,
            send_sem=send_sem.at[phase],
            recv_sem=recv_sem.at[phase],
            device_id={axis: lax.rem(me + 1, n)},
            device_id_type=MESH,
        )

    loads = [
        pltpu.make_async_copy(src, dst, local_sem.at[k])
        for k, (src, dst) in enumerate(
            (
                (store_hbm, store_ref),
                (slots_hbm, slots_ref),
                (kx_hbm, kx_ref),
                (ky_hbm, ky_ref),
                (pointwise_hbm, pointwise_ref),
                (bias_hbm, bias_ref),
                (saved_hbm, saved_ref),
                (field_hbm, field_ref),
                (cot_hbm, cot_ref),
            )
        )
    ]
    for load in loads:
        load.start()

    barrier = pltpu.get_barrier_semaphore()

    def signal_px(peer):
        pl.semaphore_signal(barrier, inc=1, device_id={"px": peer}, device_id_type=MESH)

    def greet(axis):
        n, me = (n_px, mine_x) if axis == "px" else (n_py, mine_y)

        def one(step, carry):
            pl.semaphore_signal(
                barrier, inc=1, device_id={axis: lax.rem(me + step, n)}, device_id_type=MESH
            )
            return carry

        lax.fori_loop(1, n, one, 0)

    greet("py")
    for step in STEPS:
        signal_px(lax.rem(mine_x + 2 * step, n_px))
    signal_px(sibling)

    loads[0].wait()
    loads[1].wait()
    wide = jnp.concatenate([store_ref[k] for k in range(8)], axis=1)
    piece_out[:, 0, 0:256] = wide
    piece_out[:, 0, 256:384] = jnp.zeros((n_py, 128), jnp.float32)
    piece_out[:, 0, 256:258] = jnp.broadcast_to(slots_ref[...].astype(jnp.float32), (n_py, 2))
    pl.semaphore_wait(barrier, n_py + len(STEPS))
    send(0, piece_out, piece_in, "py")

    for load in loads[2:8]:
        load.wait()
    pointwise = pointwise_ref[...]
    forward_map = spread_map(pointwise, 16, NN)
    backward_map = spread_map(pointwise, 8, NT)
    owner = iota((16 * channels, channels), 0) // 16 == iota((16 * channels, channels), 1)
    bias = jnp.sum(jnp.where(owner, bias_ref[...], 0.0), axis=1, keepdims=True)
    for part in range(2):
        cut = pl.ds(16 * part, 16)
        block = field_ref[:, cut, :].reshape(16 * channels, 512)
        mapped = jnp.dot(forward_map, block, preferred_element_type=jnp.float32) + bias
        pre_ref[:, cut, :] = mapped.reshape(channels, 16, 512)

    lane = iota((1, 128), 1)
    imag = (lane & 32) != 0
    first = lane < 64
    slot_of_lane = ((lane & 31) * 4 + (lane >> 5)).astype(jnp.float32)

    bulk(0, piece_in, "py").wait_recv()
    pieces = jnp.concatenate([piece_in[:, 0, 64 * s : 64 * s + 64] for s in range(4)], axis=0)
    slots = piece_in[:, 0, 256:384]
    selects = [
        jnp.where(slots[:, b : b + 1] == slot_of_lane, 1.0, 0.0).astype(jnp.float32)
        for b in range(2)
    ]
    chosen = jnp.concatenate([dot(select, pieces, NN, EXACT) for select in selects], axis=1)
    chosen_out[:, 0, :] = chosen
    wall_out[...] = chosen
    send(1, chosen_out, chosen_in, "py")

    saved = jnp.concatenate(
        [saved_ref[:, b, r, :] for b in range(2) for r in range(2)], axis=0
    ).T
    kx = column(kx_ref, 32, 1)
    angle_x = angle((mine_x * 32 + (iota((32, 128), 1) & 31)) * kx, full_x)
    table_x = jnp.concatenate([jnp.cos(angle_x), jnp.sin(angle_x)], axis=0) * factor
    ky = column(ky_ref, 64, 2)
    angle_y = angle(iota((64, 512), 1) * ky, 512)
    even = (iota((64, 512), 0) & 1) == 0
    table_y_ref[...] = jnp.where(even, jnp.cos(angle_y), -jnp.sin(angle_y))
    table_y = table_y_ref[...]

    bulk(1, chosen_in, "py").wait_recv()
    weights = chosen_in[:, 0, :]
    signed = jnp.where(imag, -weights, weights)
    swapped = jnp.where(imag, pltpu.roll(weights, 32, 1), pltpu.roll(weights, 96, 1))
    mix = jnp.concatenate(
        [
            jnp.where(first, signed, 0.0),
            jnp.where(first, swapped, 0.0),
            jnp.where(first, 0.0, signed),
            jnp.where(first, 0.0, swapped),
        ],
        axis=0,
    )
    mixed_out[:, 0, :] = dot(saved, mix, NT)
    send(2, mixed_out, mixed_in, "py")
    send(6, wall_out, wall_in, "py", whole=True)

    def px_copy(k, src, dst, source, peer):
        return pltpu.make_async_remote_copy(
            src_ref=src,
            dst_ref=dst,
            send_sem=send_sem.at[(3, 4, 8)[k]],
            recv_sem=px_sem.at[k, source],
            device_id={"px": peer},
            device_id_type=MESH,
        )

    def to_rows(planes, sources):
        both = jnp.concatenate(
            [
                jnp.concatenate([planes[p], turned(planes[p], imag)], axis=0)
                for p in sources
            ],
            axis=1,
        )
        rows = dot(both, table_x, TN)
        for n, p in enumerate(sources):
            rows_ref[pl.ds(pl.multiple_of(p * 128, 128), 128), :] = rows[
                128 * n : 128 * n + 128
            ]

    def scatter_plane(k, src, dst):
        px_copy(k, src, dst.at[mine_x], mine_x, sibling).start()
        for step in STEPS:
            peer = lax.rem(mine_x + 2 * step, n_px)
            px_copy(k, src, dst.at[mine_x], mine_x, peer).start()
        dst[mine_x] = src[...]

    def collect_planes(k, dst):
        def arrived(p):
            px_copy(k, dst.at[p], dst.at[p], p, sibling).wait_recv()

        arrived(sibling)
        to_rows(dst, [mine_x, sibling])
        for batch in BATCHES:
            sources = [lax.rem(mine_x + n_px - 2 * step, n_px) for step in batch]
            for p in sources:
                arrived(p)
                px_copy(k, dst.at[p], dst.at[p], p, sibling).start()
            to_rows(dst, sources)
        for batch in BATCHES:
            sources = [lax.rem(sibling + n_px - 2 * step, n_px) for step in batch]
            for p in sources:
                arrived(p)
            to_rows(dst, sources)

    bulk(2, mixed_in, "py").wait_recv()
    plane_out[...] = mixed_in[:, 0, :]
    scatter_plane(0, plane_out, plane_in)

    lane_group = lane >> 5

    def row_block(i):
        picked = rows_ref[pl.ds(4 * i, 64, stride=32), :]
        for g in range(1, 4):
            picked = jnp.where(
                lane_group == g, rows_ref[pl.ds(4 * i + g, 64, stride=32), :], picked
            )
        return dot(picked, table_y, TN)

    loads[8].wait()
    collect_planes(0, plane_in)

    def grad_block(i, carry):
        spectral = row_block(i)
        parts = []
        for g in range(4):
            o = 4 * i + g
            pre = pre_ref[o] + spectral[32 * g : 32 * g + 32]
            grad = cot_ref[o].astype(jnp.float32) * gelu_slope(pre)
            grad_ref[o] = grad
            parts.append(grad)
        freq = dot(table_y, jnp.concatenate(parts, axis=0), NT)
        for g in range(4):
            back_ref[pl.ds(4 * i + g, 64, stride=32), :] = freq
        return carry

    lax.fori_loop(0, groups, grad_block, 0, unroll=2)

    own_group = (iota((128, 128), 0) & 3) == (iota((128, 128), 1) >> 5)

    def part_tiles(targets):
        rows = jnp.concatenate(
            [
                jnp.where(
                    own_group, back_ref[pl.ds(pl.multiple_of(p * 128, 128), 128), :], 0.0
                )
                for p in targets
            ],
            axis=0,
        )
        both = dot(table_x, rows, NT)
        tiles = [both[:, 128 * n : 128 * n + 128] for n in range(len(targets))]
        return [tile[0:32] - turned(tile[32:64], imag) for tile in tiles]

    for batch in (STEPS[0:4], STEPS[4:] + (0,)):
        targets = [lax.rem(sibling + 2 * step, n_px) for step in batch]
        for p, tile in zip(targets, part_tiles(targets)):
            part_out[p] = tile
            px_copy(1, part_out.at[p], half_in.at[p], p, sibling).start()
    total = None
    for batch in (STEPS[0:4], STEPS[4:] + (0,)):
        targets = [lax.rem(mine_x + 2 * step, n_px) for step in batch]
        for step, p, tile in zip(batch, targets, part_tiles(targets)):
            px_copy(1, half_in.at[p], half_in.at[p], p, sibling).wait_recv()
            tile = tile + half_in[p]
            if step == 0:
                total = tile
            else:
                part_out[p] = tile
                pltpu.make_async_remote_copy(
                    src_ref=part_out.at[p],
                    dst_ref=part_in.at[mine_x],
                    send_sem=send_sem.at[4],
                    recv_sem=part_sem.at[mine_x],
                    device_id={"px": p},
                    device_id_type=MESH,
                ).start()

    for part in range(4):
        cut = pl.ds(8 * part, 8)
        block = grad_ref[:, cut, :].reshape(8 * channels, 512)
        upper = block.astype(jnp.bfloat16)
        lower = (block - upper.astype(jnp.float32)).astype(jnp.bfloat16)
        base = jnp.dot(backward_map, upper, preferred_element_type=jnp.float32) + jnp.dot(
            backward_map, lower, preferred_element_type=jnp.float32
        )
        pre_ref[:, cut, :] = base.reshape(channels, 8, 512)

    for step in STEPS:
        p = lax.rem(mine_x + n_px - 2 * step, n_px)
        pltpu.make_async_remote_copy(
            src_ref=part_in.at[p],
            dst_ref=part_in.at[p],
            send_sem=send_sem.at[4],
            recv_sem=part_sem.at[p],
            device_id={"px": sibling},
            device_id_type=MESH,
        ).wait_recv()
        total = total + part_in[p]
    whole_out[:, 0, :] = total
    send(5, whole_out, whole_in, "py")

    bulk(6, wall_in, "py").wait_recv()
    by_re = by_im = None
    for o in range(channels):
        wall = wall_in[o]
        re = wall * jnp.where(first, total[:, o : o + 1], total[:, 64 + o : 65 + o])
        im = wall * jnp.where(first, total[:, 32 + o : 33 + o], total[:, 96 + o : 97 + o])
        by_re = re if o == 0 else by_re + re
        by_im = im if o == 0 else by_im + im
    last_out[...] = jnp.where(
        imag, pltpu.roll(by_im, 32, 1) - by_re, by_re + pltpu.roll(by_im, 96, 1)
    )
    scatter_plane(2, last_out, last_in)

    bulk(5, whole_in, "py").wait_recv()
    spectrum_grad = whole_in[:, 0, :]
    cross = dot(spectrum_grad, saved, TN)
    blocks = None
    for b in range(2):
        re = cross[64 * b : 64 * b + 32]
        im = cross[64 * b + 32 : 64 * b + 64]
        value = jnp.where(
            imag, im_shift(im, 32) - re, re + im_shift(im, 96)
        )
        blocks = value if b == 0 else jnp.where(first, blocks, value)
    block_out[:, 0, :] = blocks
    send(7, block_out, block_in, "py")

    collect_planes(2, last_in)

    def out_block(i, carry):
        spectral = row_block(i)
        for g in range(4):
            o = 4 * i + g
            out_ref[o] = pre_ref[o] + spectral[32 * g : 32 * g + 32]
        return carry

    lax.fori_loop(0, groups // 2, out_block, 0, unroll=2)

    bulk(7, block_in, "py").wait_recv()
    received = block_in[:, 0, :]
    placed = dot(selects[0], received[:, 0:64], TN, EXACT) + dot(
        selects[1], received[:, 64:128], TN, EXACT
    )
    slot_out[:, 0, :] = jnp.concatenate([placed[32 * s : 32 * s + 32] for s in range(4)], axis=1)
    send(9, slot_out, slot_in, "py")

    lax.fori_loop(groups // 2, groups, out_block, 0, unroll=2)

    bulk(9, slot_in, "py").wait_recv()
    for k in range(8):
        store_out_ref[k] = slot_in[:, 0, 32 * k : 32 * k + 32]
    for phase, dst, axis in (
        (0, piece_in, "py"),
        (1, chosen_in, "py"),
        (2, mixed_in, "py"),
        (3, plane_in, "px"),
        (4, part_in, "px"),
        (5, whole_in, "py"),
        (6, wall_in, "py"),
        (7, block_in, "py"),
        (8, last_in, "px"),
        (9, slot_in, "py"),
    ):
        bulk(phase, dst, axis).wait_send()


def im_shift(values, amount):
    return pltpu.roll(values, amount, 1)


def on_device(
    n_px,
    n_py,
    field_in,
    cotangent,
    spectrum_saved,
    weight_store,
    block_slot,
    kx_modes,
    ky_modes,
    pointwise,
    bias_vector,
):
    channels, _, rows_x, width_y = field_in.shape
    hbm = pl.BlockSpec(memory_space=pltpu.HBM)
    f32 = jnp.float32
    row = pltpu.VMEM((n_py, 1, 128), f32)
    tile = pltpu.VMEM((32, 128), f32)
    tiles = pltpu.VMEM((n_px, 32, 128), f32)
    field_grad, store_grad = pl.pallas_call(
        functools.partial(kernel, n_px, n_py),
        out_shape=(
            pltpu.VMEM((channels, rows_x, width_y), f32),
            pltpu.VMEM((8, channels, channels), f32),
        ),
        in_specs=[hbm] * 9,
        out_specs=(pl.BlockSpec(memory_space=pltpu.VMEM),) * 2,
        scratch_shapes=[
            pltpu.VMEM((channels, rows_x, width_y), jnp.bfloat16),
            pltpu.VMEM((channels, rows_x, width_y), jnp.bfloat16),
            pltpu.VMEM((channels, 2, 2, n_py), f32),
            pltpu.VMEM((8, channels, channels), f32),
            pltpu.VMEM((1, 2), jnp.int32),
            pltpu.VMEM((1, 32), jnp.int32),
            pltpu.VMEM((1, 32), jnp.int32),
            pltpu.VMEM((channels, channels), jnp.bfloat16),
            pltpu.VMEM((1, channels), f32),
            pltpu.VMEM((64, width_y), f32),
            pltpu.VMEM((channels, rows_x, width_y), f32),
            pltpu.VMEM((channels, rows_x, width_y), f32),
            pltpu.VMEM((n_px * 128, 128), f32),
            pltpu.VMEM((n_px * 128, 128), f32),
            pltpu.VMEM((n_py, 1, 384), f32),
            pltpu.VMEM((n_py, 1, 384), f32),
            row,
            row,
            row,
            row,
            tile,
            tiles,
            tiles,
            tiles,
            tiles,
            row,
            row,
            tile,
            pltpu.VMEM((n_py, 32, 128), f32),
            tile,
            tiles,
            row,
            row,
            pltpu.VMEM((n_py, 1, 256), f32),
            pltpu.VMEM((n_py, 1, 256), f32),
            pltpu.SemaphoreType.DMA((10,)),
            pltpu.SemaphoreType.DMA((10,)),
            pltpu.SemaphoreType.DMA((3, n_px)),
            pltpu.SemaphoreType.DMA((n_px,)),
            pltpu.SemaphoreType.DMA((9,)),
        ],
        compiler_params=pltpu.CompilerParams(
            collective_id=0, has_side_effects=True, vmem_limit_bytes=48 << 20
        ),
    )(
        *held(
        field_in.reshape(channels, rows_x, width_y),
        cotangent.reshape(channels, rows_x, width_y),
        jnp.transpose(spectrum_saved[:, :, :, 0, :], (0, 2, 3, 1)),
        weight_store.reshape(8, channels, channels),
        block_slot,
        kx_modes.reshape(1, -1),
        ky_modes.reshape(1, -1),
        pointwise,
        bias_vector.reshape(1, -1),
            )
    )
    return (
        field_grad.reshape(field_in.shape),
        store_grad.reshape(weight_store.shape),
    )


def held(*arrays):
    return [pltpu.with_memory_space_constraint(array, pltpu.HBM) for array in arrays]


def solution(mesh):
    placed = (
        P(None, "py", "px", None),
        P(None, "py", "px", None),
        P(None, None, "px", "py", None),
        P(("px", "py"), None, None, None),
        P("py", "px"),
        P(),
        P(),
        P(),
        P(),
    )
    return jax.shard_map(
        functools.partial(on_device, mesh.shape["px"], mesh.shape["py"]),
        mesh=mesh,
        in_specs=placed,
        out_specs=(P(None, "py", "px", None), P(("px", "py"), None, None, None)),
        check_vma=False,
    )
```

```python
import functools
import math

import jax
import jax.numpy as jnp
from jax import lax
from jax.experimental import pallas as pl
from jax.experimental.pallas import tpu as pltpu
from jax.sharding import PartitionSpec as P

MESH = pl.DeviceIdType.MESH
HIGH = lax.Precision.HIGH
EXACT = lax.Precision.HIGHEST
NN = (((1,), (0,)), ((), ()))
NT = (((1,), (1,)), ((), ()))
TN = (((0,), (0,)), ((), ()))
STEPS = (1, 7, 2, 6, 3, 5, 4)
BATCHES = ((1, 7, 2, 6), (3, 5, 4))


def dot(a, b, dims, precision=HIGH):
    return lax.dot_general(
        a, b, dims, precision=precision, preferred_element_type=jnp.float32
    )


def gelu_slope(values):
    normal_cdf = 0.5 * (1.0 + lax.erf(values * 0.7071067811865476))
    density = jnp.exp(-0.5 * values * values) * 0.3989422804014327
    return normal_cdf + values * density


def iota(shape, axis):
    return lax.broadcasted_iota(jnp.int32, shape, axis)


def spread_map(pointwise, group, dims):
    channels = pointwise.shape[0]
    size = channels * group
    left = (iota((size, channels), 0) // group == iota((size, channels), 1)).astype(jnp.bfloat16)
    right = (iota((channels, size), 1) // group == iota((channels, size), 0)).astype(jnp.bfloat16)
    half = lax.dot_general(left, pointwise, dims, preferred_element_type=jnp.float32)
    full = jnp.dot(half.astype(jnp.bfloat16), right, preferred_element_type=jnp.float32)
    same = (iota((size, size), 0) & (group - 1)) == (iota((size, size), 1) & (group - 1))
    return jnp.where(same, full, 0.0).astype(jnp.bfloat16)


def column(row_ref, size, repeat):
    count = row_ref.shape[1]
    same = iota((size, count), 0) // repeat == iota((size, count), 1)
    row = row_ref[...].astype(jnp.float32)
    return jnp.sum(jnp.where(same, row, 0.0), axis=1, keepdims=True).astype(jnp.int32)


def angle(points, length):
    return (points & (length - 1)).astype(jnp.float32) * (2.0 * math.pi / length)


def turned(values, imag):
    return jnp.where(imag, pltpu.roll(values, 32, 1), -pltpu.roll(values, 96, 1))


def kernel(
    n_px,
    n_py,
    field_hbm,
    cot_hbm,
    saved_hbm,
    store_hbm,
    slots_hbm,
    kx_hbm,
    ky_hbm,
    pointwise_hbm,
    bias_hbm,
    out_ref,
    store_out_ref,
    field_ref,
    cot_ref,
    saved_ref,
    store_ref,
    slots_ref,
    kx_ref,
    ky_ref,
    pointwise_ref,
    bias_ref,
    table_y_ref,
    pre_ref,
    grad_ref,
    rows_ref,
    back_ref,
    piece_out,
    piece_in,
    chosen_out,
    chosen_in,
    mixed_out,
    mixed_in,
    plane_out,
    plane_in,
    part_out,
    part_in,
    half_in,
    whole_out,
    whole_in,
    wall_out,
    wall_in,
    last_out,
    last_in,
    saved_out,
    saved_in,
    sums_ref,
    slot_out,
    slot_in,
    send_sem,
    recv_sem,
    px_sem,
    part_sem,
    local_sem,
):
    mine_x = lax.axis_index("px")
    mine_y = lax.axis_index("py")
    sibling = mine_x + 1 - 2 * lax.rem(mine_x, 2)
    full_x = 32 * n_px
    factor = 1.0 / math.sqrt(full_x * 512)
    channels = 32
    groups = channels // 4

    def send(phase, src, dst, axis, whole=False):
        n, me = (n_px, mine_x) if axis == "px" else (n_py, mine_y)

        def one(step, carry):
            peer = lax.rem(me + step, n)
            pltpu.make_async_remote_copy(
                src_ref=src if whole else src.at[peer],
                dst_ref=dst.at[me],
                send_sem=send_sem.at[phase],
                recv_sem=recv_sem.at[phase],
                device_id={axis: peer},
                device_id_type=MESH,
            ).start()
            return carry

        lax.fori_loop(1, n, one, 0)
        dst[me] = src[...] if whole else src[me]

    def bulk(phase, dst, axis):
        n, me = (n_px, mine_x) if axis == "px" else (n_py, mine_y)
        span = dst.at[pl.ds(0, n - 1)]
        return pltpu.make_async_remote_copy(
            src_ref=span,
            dst_ref=span,
            send_sem=send_sem.at[phase],
            recv_sem=recv_sem.at[phase],
            device_id={axis: lax.rem(me + 1, n)},
            device_id_type=MESH,
        )

    loads = [
        pltpu.make_async_copy(src, dst, local_sem.at[k])
        for k, (src, dst) in enumerate(
            (
                (store_hbm, store_ref),
                (slots_hbm, slots_ref),
                (kx_hbm, kx_ref),
                (ky_hbm, ky_ref),
                (pointwise_hbm, pointwise_ref),
                (bias_hbm, bias_ref),
                (saved_hbm, saved_ref),
                (field_hbm, field_ref),
                (cot_hbm, cot_ref),
            )
        )
    ]
    for load in loads:
        load.start()

    barrier = pltpu.get_barrier_semaphore()

    def signal_px(peer):
        pl.semaphore_signal(barrier, inc=1, device_id={"px": peer}, device_id_type=MESH)

    def greet(axis):
        n, me = (n_px, mine_x) if axis == "px" else (n_py, mine_y)

        def one(step, carry):
            pl.semaphore_signal(
                barrier, inc=1, device_id={axis: lax.rem(me + step, n)}, device_id_type=MESH
            )
            return carry

        lax.fori_loop(1, n, one, 0)

    greet("py")
    for step in STEPS:
        signal_px(lax.rem(mine_x + 2 * step, n_px))
    signal_px(sibling)

    loads[0].wait()
    loads[1].wait()
    wide = jnp.concatenate([store_ref[k] for k in range(8)], axis=1)
    piece_out[:, 0, 0:256] = wide
    piece_out[:, 0, 256:384] = jnp.zeros((n_py, 128), jnp.float32)
    piece_out[:, 0, 256:258] = jnp.broadcast_to(slots_ref[...].astype(jnp.float32), (n_py, 2))
    pl.semaphore_wait(barrier, n_py + len(STEPS))
    send(0, piece_out, piece_in, "py")

    for load in loads[2:8]:
        load.wait()
    pointwise = pointwise_ref[...]
    forward_map = spread_map(pointwise, 16, NN)
    backward_map = spread_map(pointwise, 8, NT)
    owner = iota((16 * channels, channels), 0) // 16 == iota((16 * channels, channels), 1)
    bias = jnp.sum(jnp.where(owner, bias_ref[...], 0.0), axis=1, keepdims=True)
    for part in range(2):
        cut = pl.ds(16 * part, 16)
        block = field_ref[:, cut, :].reshape(16 * channels, 512)
        mapped = jnp.dot(forward_map, block, preferred_element_type=jnp.float32) + bias
        pre_ref[:, cut, :] = mapped.reshape(channels, 16, 512)

    lane = iota((1, 128), 1)
    imag = (lane & 32) != 0
    first = lane < 64
    slot_of_lane = ((lane & 31) * 4 + (lane >> 5)).astype(jnp.float32)

    bulk(0, piece_in, "py").wait_recv()
    pieces = jnp.concatenate([piece_in[:, 0, 64 * s : 64 * s + 64] for s in range(4)], axis=0)
    slots = piece_in[:, 0, 256:384]
    selects = [
        jnp.where(slots[:, b : b + 1] == slot_of_lane, 1.0, 0.0).astype(jnp.float32)
        for b in range(2)
    ]
    chosen = jnp.concatenate([dot(select, pieces, NN, EXACT) for select in selects], axis=1)
    chosen_out[:, 0, :] = chosen
    wall_out[...] = chosen
    send(1, chosen_out, chosen_in, "py")

    saved = jnp.concatenate(
        [saved_ref[:, b, r, :] for b in range(2) for r in range(2)], axis=0
    ).T
    saved_out[...] = saved
    kx = column(kx_ref, 32, 1)
    angle_x = angle((mine_x * 32 + (iota((32, 128), 1) & 31)) * kx, full_x)
    table_x = jnp.concatenate([jnp.cos(angle_x), jnp.sin(angle_x)], axis=0) * factor
    ky = column(ky_ref, 64, 2)
    angle_y = angle(iota((64, 512), 1) * ky, 512)
    even = (iota((64, 512), 0) & 1) == 0
    table_y_ref[...] = jnp.where(even, jnp.cos(angle_y), -jnp.sin(angle_y))
    table_y = table_y_ref[...]

    bulk(1, chosen_in, "py").wait_recv()
    weights = chosen_in[:, 0, :]
    signed = jnp.where(imag, -weights, weights)
    swapped = jnp.where(imag, pltpu.roll(weights, 32, 1), pltpu.roll(weights, 96, 1))
    mix = jnp.concatenate(
        [
            jnp.where(first, signed, 0.0),
            jnp.where(first, swapped, 0.0),
            jnp.where(first, 0.0, signed),
            jnp.where(first, 0.0, swapped),
        ],
        axis=0,
    )
    mixed_out[:, 0, :] = dot(saved, mix, NT)
    send(2, mixed_out, mixed_in, "py")
    send(6, wall_out, wall_in, "py", whole=True)

    def px_copy(k, src, dst, source, peer):
        return pltpu.make_async_remote_copy(
            src_ref=src,
            dst_ref=dst,
            send_sem=send_sem.at[(3, 4, 8)[k]],
            recv_sem=px_sem.at[k, source],
            device_id={"px": peer},
            device_id_type=MESH,
        )

    def to_rows(planes, sources):
        both = jnp.concatenate(
            [
                jnp.concatenate([planes[p], turned(planes[p], imag)], axis=0)
                for p in sources
            ],
            axis=1,
        )
        rows = dot(both, table_x, TN)
        for n, p in enumerate(sources):
            rows_ref[pl.ds(pl.multiple_of(p * 128, 128), 128), :] = rows[
                128 * n : 128 * n + 128
            ]

    def scatter_plane(k, src, dst):
        px_copy(k, src, dst.at[mine_x], mine_x, sibling).start()
        for step in STEPS:
            peer = lax.rem(mine_x + 2 * step, n_px)
            px_copy(k, src, dst.at[mine_x], mine_x, peer).start()
        dst[mine_x] = src[...]

    def collect_planes(k, dst):
        def arrived(p):
            px_copy(k, dst.at[p], dst.at[p], p, sibling).wait_recv()

        arrived(sibling)
        to_rows(dst, [mine_x, sibling])
        for batch in BATCHES:
            sources = [lax.rem(mine_x + n_px - 2 * step, n_px) for step in batch]
            for p in sources:
                arrived(p)
                px_copy(k, dst.at[p], dst.at[p], p, sibling).start()
            to_rows(dst, sources)
        for batch in BATCHES:
            sources = [lax.rem(sibling + n_px - 2 * step, n_px) for step in batch]
            for p in sources:
                arrived(p)
            to_rows(dst, sources)

    bulk(2, mixed_in, "py").wait_recv()
    plane_out[...] = mixed_in[:, 0, :]
    scatter_plane(0, plane_out, plane_in)
    send(7, saved_out, saved_in, "py", whole=True)

    lane_group = lane >> 5

    def row_block(i):
        picked = rows_ref[pl.ds(4 * i, 64, stride=32), :]
        for g in range(1, 4):
            picked = jnp.where(
                lane_group == g, rows_ref[pl.ds(4 * i + g, 64, stride=32), :], picked
            )
        return dot(picked, table_y, TN)

    loads[8].wait()
    collect_planes(0, plane_in)

    def grad_block(i, carry):
        spectral = row_block(i)
        parts = []
        for g in range(4):
            o = 4 * i + g
            pre = pre_ref[o] + spectral[32 * g : 32 * g + 32]
            grad = cot_ref[o].astype(jnp.float32) * gelu_slope(pre)
            grad_ref[o] = grad
            parts.append(grad)
        freq = dot(table_y, jnp.concatenate(parts, axis=0), NT)
        for g in range(4):
            back_ref[pl.ds(4 * i + g, 64, stride=32), :] = freq
        return carry

    lax.fori_loop(0, groups, grad_block, 0, unroll=2)

    own_group = (iota((128, 128), 0) & 3) == (iota((128, 128), 1) >> 5)

    def part_tiles(targets):
        rows = jnp.concatenate(
            [
                jnp.where(
                    own_group, back_ref[pl.ds(pl.multiple_of(p * 128, 128), 128), :], 0.0
                )
                for p in targets
            ],
            axis=0,
        )
        both = dot(table_x, rows, NT)
        tiles = [both[:, 128 * n : 128 * n + 128] for n in range(len(targets))]
        return [tile[0:32] - turned(tile[32:64], imag) for tile in tiles]

    for batch in (STEPS[0:4], STEPS[4:] + (0,)):
        targets = [lax.rem(sibling + 2 * step, n_px) for step in batch]
        for p, tile in zip(targets, part_tiles(targets)):
            part_out[p] = tile
            px_copy(1, part_out.at[p], half_in.at[p], p, sibling).start()
    total = None
    for batch in (STEPS[0:4], STEPS[4:] + (0,)):
        targets = [lax.rem(mine_x + 2 * step, n_px) for step in batch]
        for step, p, tile in zip(batch, targets, part_tiles(targets)):
            px_copy(1, half_in.at[p], half_in.at[p], p, sibling).wait_recv()
            tile = tile + half_in[p]
            if step == 0:
                total = tile
            else:
                part_out[p] = tile
                pltpu.make_async_remote_copy(
                    src_ref=part_out.at[p],
                    dst_ref=part_in.at[mine_x],
                    send_sem=send_sem.at[4],
                    recv_sem=part_sem.at[mine_x],
                    device_id={"px": p},
                    device_id_type=MESH,
                ).start()

    for part in range(4):
        cut = pl.ds(8 * part, 8)
        block = grad_ref[:, cut, :].reshape(8 * channels, 512)
        upper = block.astype(jnp.bfloat16)
        lower = (block - upper.astype(jnp.float32)).astype(jnp.bfloat16)
        base = jnp.dot(backward_map, upper, preferred_element_type=jnp.float32) + jnp.dot(
            backward_map, lower, preferred_element_type=jnp.float32
        )
        pre_ref[:, cut, :] = base.reshape(channels, 8, 512)

    for step in STEPS:
        p = lax.rem(mine_x + n_px - 2 * step, n_px)
        pltpu.make_async_remote_copy(
            src_ref=part_in.at[p],
            dst_ref=part_in.at[p],
            send_sem=send_sem.at[4],
            recv_sem=part_sem.at[p],
            device_id={"px": sibling},
            device_id_type=MESH,
        ).wait_recv()
        total = total + part_in[p]
    turned_total = total.T
    whole_out[:, 0, :] = jnp.concatenate(
        [turned_total[32 * k : 32 * k + 32] for k in range(4)], axis=1
    )
    send(5, whole_out, whole_in, "py")

    def pair(rows, k):
        return jnp.where(first, rows[:, k : k + 1], rows[:, 64 + k : 65 + k])

    def crossed(by_re, by_im):
        return jnp.where(
            imag, pltpu.roll(by_im, 32, 1) - by_re, by_re + pltpu.roll(by_im, 96, 1)
        )

    bulk(6, wall_in, "py").wait_recv()
    def wall_step(o, carry):
        rows, by_re, by_im = carry
        wall = wall_in[o]
        return (
            pltpu.roll(rows, 127, 1),
            by_re + wall * pair(rows, 0),
            by_im + wall * pair(rows, 32),
        )

    zero = jnp.zeros((32, 128), jnp.float32)
    _, by_re, by_im = lax.fori_loop(0, channels, wall_step, (total, zero, zero), unroll=4)
    last_out[...] = crossed(by_re, by_im)
    scatter_plane(2, last_out, last_in)

    bulk(5, whole_in, "py").wait_recv()
    bulk(7, saved_in, "py").wait_recv()
    grads = whole_in[:, 0, :]

    def saved_step(k, grads):
        inputs = saved_in[k]
        for part in range(2):
            sums = jnp.sum(inputs * pair(grads, 32 * part), axis=0, keepdims=True)
            sums_ref[part, pl.ds(k, 1), :] = sums
        return pltpu.roll(grads, 127, 1)

    lax.fori_loop(0, 32, saved_step, grads, unroll=4)
    received = crossed(sums_ref[0], sums_ref[1])
    placed = dot(selects[0], received[:, 0:64], TN, EXACT) + dot(
        selects[1], received[:, 64:128], TN, EXACT
    )
    slot_out[:, 0, :] = jnp.concatenate([placed[32 * s : 32 * s + 32] for s in range(4)], axis=1)
    send(9, slot_out, slot_in, "py")

    collect_planes(2, last_in)

    def out_block(i, carry):
        spectral = row_block(i)
        for g in range(4):
            o = 4 * i + g
            out_ref[o] = pre_ref[o] + spectral[32 * g : 32 * g + 32]
        return carry

    lax.fori_loop(0, groups, out_block, 0, unroll=2)

    bulk(9, slot_in, "py").wait_recv()
    for k in range(8):
        store_out_ref[k] = slot_in[:, 0, 32 * k : 32 * k + 32]
    for phase, dst, axis in (
        (0, piece_in, "py"),
        (1, chosen_in, "py"),
        (2, mixed_in, "py"),
        (3, plane_in, "px"),
        (4, part_in, "px"),
        (5, whole_in, "py"),
        (6, wall_in, "py"),
        (7, saved_in, "py"),
        (8, last_in, "px"),
        (9, slot_in, "py"),
    ):
        bulk(phase, dst, axis).wait_send()


def on_device(
    n_px,
    n_py,
    field_in,
    cotangent,
    spectrum_saved,
    weight_store,
    block_slot,
    kx_modes,
    ky_modes,
    pointwise,
    bias_vector,
):
    channels, _, rows_x, width_y = field_in.shape
    hbm = pl.BlockSpec(memory_space=pltpu.HBM)
    f32 = jnp.float32
    row = pltpu.VMEM((n_py, 1, 128), f32)
    tile = pltpu.VMEM((32, 128), f32)
    tiles = pltpu.VMEM((n_px, 32, 128), f32)
    field_grad, store_grad = pl.pallas_call(
        functools.partial(kernel, n_px, n_py),
        out_shape=(
            pltpu.VMEM((channels, rows_x, width_y), f32),
            pltpu.VMEM((8, channels, channels), f32),
        ),
        in_specs=[hbm] * 9,
        out_specs=(pl.BlockSpec(memory_space=pltpu.VMEM),) * 2,
        scratch_shapes=[
            pltpu.VMEM((channels, rows_x, width_y), jnp.bfloat16),
            pltpu.VMEM((channels, rows_x, width_y), jnp.bfloat16),
            pltpu.VMEM((channels, 2, 2, n_py), f32),
            pltpu.VMEM((8, channels, channels), f32),
            pltpu.VMEM((1, 2), jnp.int32),
            pltpu.VMEM((1, 32), jnp.int32),
            pltpu.VMEM((1, 32), jnp.int32),
            pltpu.VMEM((channels, channels), jnp.bfloat16),
            pltpu.VMEM((1, channels), f32),
            pltpu.VMEM((64, width_y), f32),
            pltpu.VMEM((channels, rows_x, width_y), f32),
            pltpu.VMEM((channels, rows_x, width_y), f32),
            pltpu.VMEM((n_px * 128, 128), f32),
            pltpu.VMEM((n_px * 128, 128), f32),
            pltpu.VMEM((n_py, 1, 384), f32),
            pltpu.VMEM((n_py, 1, 384), f32),
            row,
            row,
            row,
            row,
            tile,
            tiles,
            tiles,
            tiles,
            tiles,
            row,
            row,
            tile,
            pltpu.VMEM((n_py, 32, 128), f32),
            tile,
            tiles,
            tile,
            pltpu.VMEM((n_py, 32, 128), f32),
            pltpu.VMEM((2, 32, 128), f32),
            pltpu.VMEM((n_py, 1, 256), f32),
            pltpu.VMEM((n_py, 1, 256), f32),
            pltpu.SemaphoreType.DMA((10,)),
            pltpu.SemaphoreType.DMA((10,)),
            pltpu.SemaphoreType.DMA((3, n_px)),
            pltpu.SemaphoreType.DMA((n_px,)),
            pltpu.SemaphoreType.DMA((9,)),
        ],
        compiler_params=pltpu.CompilerParams(
            collective_id=0, has_side_effects=True, vmem_limit_bytes=48 << 20
        ),
    )(
        *held(
        field_in.reshape(channels, rows_x, width_y),
        cotangent.reshape(channels, rows_x, width_y),
        jnp.transpose(spectrum_saved[:, :, :, 0, :], (0, 2, 3, 1)),
        weight_store.reshape(8, channels, channels),
        block_slot,
        kx_modes.reshape(1, -1),
        ky_modes.reshape(1, -1),
        pointwise,
        bias_vector.reshape(1, -1),
            )
    )
    return (
        field_grad.reshape(field_in.shape),
        store_grad.reshape(weight_store.shape),
    )


def held(*arrays):
    return [pltpu.with_memory_space_constraint(array, pltpu.HBM) for array in arrays]


def solution(mesh):
    placed = (
        P(None, "py", "px", None),
        P(None, "py", "px", None),
        P(None, None, "px", "py", None),
        P(("px", "py"), None, None, None),
        P("py", "px"),
        P(),
        P(),
        P(),
        P(),
    )
    return jax.shard_map(
        functools.partial(on_device, mesh.shape["px"], mesh.shape["py"]),
        mesh=mesh,
        in_specs=placed,
        out_specs=(P(None, "py", "px", None), P(("px", "py"), None, None, None)),
        check_vma=False,
    )
```

```python
import functools
import math

import jax
import jax.numpy as jnp
from jax import lax
from jax.experimental import pallas as pl
from jax.experimental.pallas import tpu as pltpu
from jax.sharding import PartitionSpec as P

MESH = pl.DeviceIdType.MESH
HIGH = lax.Precision.HIGH
EXACT = lax.Precision.HIGHEST
NN = (((1,), (0,)), ((), ()))
NT = (((1,), (1,)), ((), ()))
TN = (((0,), (0,)), ((), ()))
STEPS = (1, 7, 2, 6, 3, 5, 4)
BATCHES = ((1, 7, 2, 6), (3, 5, 4))


def dot(a, b, dims, precision=HIGH):
    return lax.dot_general(
        a, b, dims, precision=precision, preferred_element_type=jnp.float32
    )


def gelu_slope(values):
    normal_cdf = 0.5 * (1.0 + lax.erf(values * 0.7071067811865476))
    density = jnp.exp(-0.5 * values * values) * 0.3989422804014327
    return normal_cdf + values * density


def iota(shape, axis):
    return lax.broadcasted_iota(jnp.int32, shape, axis)


def spread_map(pointwise, group, dims):
    channels = pointwise.shape[0]
    size = channels * group
    left = (iota((size, channels), 0) // group == iota((size, channels), 1)).astype(jnp.bfloat16)
    right = (iota((channels, size), 1) // group == iota((channels, size), 0)).astype(jnp.bfloat16)
    half = lax.dot_general(left, pointwise, dims, preferred_element_type=jnp.float32)
    full = jnp.dot(half.astype(jnp.bfloat16), right, preferred_element_type=jnp.float32)
    same = (iota((size, size), 0) & (group - 1)) == (iota((size, size), 1) & (group - 1))
    return jnp.where(same, full, 0.0).astype(jnp.bfloat16)


def column(row_ref, size, repeat):
    count = row_ref.shape[1]
    same = iota((size, count), 0) // repeat == iota((size, count), 1)
    row = row_ref[...].astype(jnp.float32)
    return jnp.sum(jnp.where(same, row, 0.0), axis=1, keepdims=True).astype(jnp.int32)


def angle(points, length):
    return (points & (length - 1)).astype(jnp.float32) * (2.0 * math.pi / length)


def turned(values, imag):
    return jnp.where(imag, pltpu.roll(values, 32, 1), -pltpu.roll(values, 96, 1))


def kernel(
    n_px,
    n_py,
    field_hbm,
    cot_hbm,
    saved_hbm,
    store_hbm,
    slots_hbm,
    kx_hbm,
    ky_hbm,
    pointwise_hbm,
    bias_hbm,
    out_ref,
    store_out_ref,
    field_ref,
    cot_ref,
    saved_ref,
    store_ref,
    slots_ref,
    kx_ref,
    ky_ref,
    pointwise_ref,
    bias_ref,
    table_y_ref,
    pre_ref,
    grad_ref,
    rows_ref,
    back_ref,
    piece_out,
    piece_in,
    chosen_out,
    chosen_in,
    mixed_out,
    mixed_in,
    plane_out,
    plane_in,
    part_out,
    part_in,
    half_in,
    whole_out,
    whole_in,
    wall_out,
    wall_in,
    last_out,
    last_in,
    saved_out,
    saved_in,
    sums_ref,
    slot_out,
    slot_in,
    send_sem,
    recv_sem,
    px_sem,
    part_sem,
    local_sem,
):
    mine_x = lax.axis_index("px")
    mine_y = lax.axis_index("py")
    sibling = mine_x + 1 - 2 * lax.rem(mine_x, 2)
    full_x = 32 * n_px
    factor = 1.0 / math.sqrt(full_x * 512)
    channels = 32
    groups = channels // 4

    def send(phase, src, dst, axis, whole=False):
        n, me = (n_px, mine_x) if axis == "px" else (n_py, mine_y)

        def one(step, carry):
            peer = lax.rem(me + step, n)
            pltpu.make_async_remote_copy(
                src_ref=src if whole else src.at[peer],
                dst_ref=dst.at[me],
                send_sem=send_sem.at[phase],
                recv_sem=recv_sem.at[phase],
                device_id={axis: peer},
                device_id_type=MESH,
            ).start()
            return carry

        lax.fori_loop(1, n, one, 0)
        dst[me] = src[...] if whole else src[me]

    def bulk(phase, dst, axis):
        n, me = (n_px, mine_x) if axis == "px" else (n_py, mine_y)
        span = dst.at[pl.ds(0, n - 1)]
        return pltpu.make_async_remote_copy(
            src_ref=span,
            dst_ref=span,
            send_sem=send_sem.at[phase],
            recv_sem=recv_sem.at[phase],
            device_id={axis: lax.rem(me + 1, n)},
            device_id_type=MESH,
        )

    loads = [
        pltpu.make_async_copy(src, dst, local_sem.at[k])
        for k, (src, dst) in enumerate(
            (
                (store_hbm, store_ref),
                (slots_hbm, slots_ref),
                (kx_hbm, kx_ref),
                (ky_hbm, ky_ref),
                (pointwise_hbm, pointwise_ref),
                (bias_hbm, bias_ref),
                (saved_hbm, saved_ref),
                (field_hbm, field_ref),
                (cot_hbm, cot_ref),
            )
        )
    ]
    for load in loads:
        load.start()

    barrier = pltpu.get_barrier_semaphore()

    def signal_px(peer):
        pl.semaphore_signal(barrier, inc=1, device_id={"px": peer}, device_id_type=MESH)

    def greet(axis):
        n, me = (n_px, mine_x) if axis == "px" else (n_py, mine_y)

        def one(step, carry):
            pl.semaphore_signal(
                barrier, inc=1, device_id={axis: lax.rem(me + step, n)}, device_id_type=MESH
            )
            return carry

        lax.fori_loop(1, n, one, 0)

    greet("py")
    for step in STEPS:
        signal_px(lax.rem(mine_x + 2 * step, n_px))
    signal_px(sibling)

    loads[0].wait()
    loads[1].wait()
    wide = jnp.concatenate([store_ref[k] for k in range(8)], axis=1)
    piece_out[:, 0, 0:256] = wide
    piece_out[:, 0, 256:384] = jnp.zeros((n_py, 128), jnp.float32)
    piece_out[:, 0, 256:258] = jnp.broadcast_to(slots_ref[...].astype(jnp.float32), (n_py, 2))
    pl.semaphore_wait(barrier, n_py + len(STEPS))
    send(0, piece_out, piece_in, "py")

    for load in loads[2:8]:
        load.wait()
    pointwise = pointwise_ref[...]
    forward_map = spread_map(pointwise, 16, NN)
    backward_map = spread_map(pointwise, 8, NT)
    owner = iota((16 * channels, channels), 0) // 16 == iota((16 * channels, channels), 1)
    bias = jnp.sum(jnp.where(owner, bias_ref[...], 0.0), axis=1, keepdims=True)
    for part in range(2):
        cut = pl.ds(16 * part, 16)
        block = field_ref[:, cut, :].reshape(16 * channels, 512)
        mapped = jnp.dot(forward_map, block, preferred_element_type=jnp.float32) + bias
        pre_ref[:, cut, :] = mapped.reshape(channels, 16, 512)

    lane = iota((1, 128), 1)
    imag = (lane & 32) != 0
    first = lane < 64
    slot_of_lane = ((lane & 31) * 4 + (lane >> 5)).astype(jnp.float32)

    bulk(0, piece_in, "py").wait_recv()
    pieces = jnp.concatenate([piece_in[:, 0, 64 * s : 64 * s + 64] for s in range(4)], axis=0)
    slots = piece_in[:, 0, 256:384]
    selects = [
        jnp.where(slots[:, b : b + 1] == slot_of_lane, 1.0, 0.0).astype(jnp.float32)
        for b in range(2)
    ]
    chosen = jnp.concatenate([dot(select, pieces, NN, EXACT) for select in selects], axis=1)
    chosen_out[:, 0, :] = chosen
    wall_out[...] = chosen
    send(1, chosen_out, chosen_in, "py")

    saved = jnp.concatenate(
        [saved_ref[:, b, r, :] for b in range(2) for r in range(2)], axis=0
    ).T
    saved_out[...] = saved
    kx = column(kx_ref, 32, 1)
    angle_x = angle((mine_x * 32 + (iota((32, 128), 1) & 31)) * kx, full_x)
    table_x = jnp.concatenate([jnp.cos(angle_x), jnp.sin(angle_x)], axis=0) * factor
    ky = column(ky_ref, 64, 2)
    angle_y = angle(iota((64, 512), 1) * ky, 512)
    even = (iota((64, 512), 0) & 1) == 0
    table_y_ref[...] = jnp.where(even, jnp.cos(angle_y), -jnp.sin(angle_y))
    table_y = table_y_ref[...]

    bulk(1, chosen_in, "py").wait_recv()
    weights = chosen_in[:, 0, :]
    signed = jnp.where(imag, -weights, weights)
    swapped = jnp.where(imag, pltpu.roll(weights, 32, 1), pltpu.roll(weights, 96, 1))
    mix = jnp.concatenate(
        [
            jnp.where(first, signed, 0.0),
            jnp.where(first, swapped, 0.0),
            jnp.where(first, 0.0, signed),
            jnp.where(first, 0.0, swapped),
        ],
        axis=0,
    )
    mixed_out[:, 0, :] = dot(saved, mix, NT)
    send(2, mixed_out, mixed_in, "py")
    send(6, wall_out, wall_in, "py", whole=True)

    def px_copy(k, src, dst, source, peer):
        return pltpu.make_async_remote_copy(
            src_ref=src,
            dst_ref=dst,
            send_sem=send_sem.at[(3, 4, 8)[k]],
            recv_sem=px_sem.at[k, source],
            device_id={"px": peer},
            device_id_type=MESH,
        )

    def to_rows(planes, sources):
        both = jnp.concatenate(
            [
                jnp.concatenate([planes[p], turned(planes[p], imag)], axis=0)
                for p in sources
            ],
            axis=1,
        )
        rows = dot(both, table_x, TN)
        for n, p in enumerate(sources):
            rows_ref[pl.ds(pl.multiple_of(p * 128, 128), 128), :] = rows[
                128 * n : 128 * n + 128
            ]

    def scatter_plane(k, src, dst):
        px_copy(k, src, dst.at[mine_x], mine_x, sibling).start()
        for step in STEPS:
            peer = lax.rem(mine_x + 2 * step, n_px)
            px_copy(k, src, dst.at[mine_x], mine_x, peer).start()
        dst[mine_x] = src[...]

    def collect_planes(k, dst):
        def arrived(p):
            px_copy(k, dst.at[p], dst.at[p], p, sibling).wait_recv()

        arrived(sibling)
        to_rows(dst, [mine_x, sibling])
        for batch in BATCHES:
            sources = [lax.rem(mine_x + n_px - 2 * step, n_px) for step in batch]
            for p in sources:
                arrived(p)
                px_copy(k, dst.at[p], dst.at[p], p, sibling).start()
            to_rows(dst, sources)
        for batch in BATCHES:
            sources = [lax.rem(sibling + n_px - 2 * step, n_px) for step in batch]
            for p in sources:
                arrived(p)
            to_rows(dst, sources)

    bulk(2, mixed_in, "py").wait_recv()
    plane_out[...] = mixed_in[:, 0, :]
    scatter_plane(0, plane_out, plane_in)
    send(7, saved_out, saved_in, "py", whole=True)

    lane_group = lane >> 5

    def row_block(i):
        picked = rows_ref[pl.ds(4 * i, 64, stride=32), :]
        for g in range(1, 4):
            picked = jnp.where(
                lane_group == g, rows_ref[pl.ds(4 * i + g, 64, stride=32), :], picked
            )
        return dot(picked, table_y, TN)

    loads[8].wait()
    collect_planes(0, plane_in)

    def grad_block(i, carry):
        spectral = row_block(i)
        parts = []
        for g in range(4):
            o = 4 * i + g
            pre = pre_ref[o] + spectral[32 * g : 32 * g + 32]
            grad = cot_ref[o].astype(jnp.float32) * gelu_slope(pre)
            grad_ref[o] = grad
            parts.append(grad)
        freq = dot(table_y, jnp.concatenate(parts, axis=0), NT)
        for g in range(4):
            back_ref[pl.ds(4 * i + g, 64, stride=32), :] = freq
        return carry

    lax.fori_loop(0, groups, grad_block, 0, unroll=4)

    own_group = (iota((128, 128), 0) & 3) == (iota((128, 128), 1) >> 5)

    def part_tiles(targets):
        rows = jnp.concatenate(
            [
                jnp.where(
                    own_group, back_ref[pl.ds(pl.multiple_of(p * 128, 128), 128), :], 0.0
                )
                for p in targets
            ],
            axis=0,
        )
        both = dot(table_x, rows, NT)
        tiles = [both[:, 128 * n : 128 * n + 128] for n in range(len(targets))]
        return [tile[0:32] - turned(tile[32:64], imag) for tile in tiles]

    for batch in (STEPS[0:4], STEPS[4:] + (0,)):
        targets = [lax.rem(sibling + 2 * step, n_px) for step in batch]
        for p, tile in zip(targets, part_tiles(targets)):
            part_out[p] = tile
            px_copy(1, part_out.at[p], half_in.at[p], p, sibling).start()
    total = None
    for batch in (STEPS[0:4], STEPS[4:] + (0,)):
        targets = [lax.rem(mine_x + 2 * step, n_px) for step in batch]
        for step, p, tile in zip(batch, targets, part_tiles(targets)):
            px_copy(1, half_in.at[p], half_in.at[p], p, sibling).wait_recv()
            tile = tile + half_in[p]
            if step == 0:
                total = tile
            else:
                part_out[p] = tile
                pltpu.make_async_remote_copy(
                    src_ref=part_out.at[p],
                    dst_ref=part_in.at[mine_x],
                    send_sem=send_sem.at[4],
                    recv_sem=part_sem.at[mine_x],
                    device_id={"px": p},
                    device_id_type=MESH,
                ).start()

    for part in range(4):
        cut = pl.ds(8 * part, 8)
        block = grad_ref[:, cut, :].reshape(8 * channels, 512)
        upper = block.astype(jnp.bfloat16)
        lower = (block - upper.astype(jnp.float32)).astype(jnp.bfloat16)
        base = jnp.dot(backward_map, upper, preferred_element_type=jnp.float32) + jnp.dot(
            backward_map, lower, preferred_element_type=jnp.float32
        )
        pre_ref[:, cut, :] = base.reshape(channels, 8, 512)

    for step in STEPS:
        p = lax.rem(mine_x + n_px - 2 * step, n_px)
        pltpu.make_async_remote_copy(
            src_ref=part_in.at[p],
            dst_ref=part_in.at[p],
            send_sem=send_sem.at[4],
            recv_sem=part_sem.at[p],
            device_id={"px": sibling},
            device_id_type=MESH,
        ).wait_recv()
        total = total + part_in[p]
    turned_total = total.T
    whole_out[:, 0, :] = jnp.concatenate(
        [turned_total[32 * k : 32 * k + 32] for k in range(4)], axis=1
    )
    send(5, whole_out, whole_in, "py")

    def pair(rows, k):
        return jnp.where(first, rows[:, k : k + 1], rows[:, 64 + k : 65 + k])

    def crossed(by_re, by_im):
        return jnp.where(
            imag, pltpu.roll(by_im, 32, 1) - by_re, by_re + pltpu.roll(by_im, 96, 1)
        )

    bulk(6, wall_in, "py").wait_recv()
    def wall_step(o, carry):
        rows, by_re, by_im = carry
        wall = wall_in[o]
        return (
            pltpu.roll(rows, 127, 1),
            by_re + wall * pair(rows, 0),
            by_im + wall * pair(rows, 32),
        )

    zero = jnp.zeros((32, 128), jnp.float32)
    _, by_re, by_im = lax.fori_loop(0, channels, wall_step, (total, zero, zero), unroll=4)
    last_out[...] = crossed(by_re, by_im)
    scatter_plane(2, last_out, last_in)

    bulk(5, whole_in, "py").wait_recv()
    bulk(7, saved_in, "py").wait_recv()
    grads = whole_in[:, 0, :]

    def saved_step(k, grads):
        inputs = saved_in[k]
        for part in range(2):
            sums = jnp.sum(inputs * pair(grads, 32 * part), axis=0, keepdims=True)
            sums_ref[part, pl.ds(k, 1), :] = sums
        return pltpu.roll(grads, 127, 1)

    lax.fori_loop(0, 32, saved_step, grads, unroll=4)
    received = crossed(sums_ref[0], sums_ref[1])
    placed = dot(selects[0], received[:, 0:64], TN, EXACT) + dot(
        selects[1], received[:, 64:128], TN, EXACT
    )
    slot_out[:, 0, :] = jnp.concatenate([placed[32 * s : 32 * s + 32] for s in range(4)], axis=1)
    send(9, slot_out, slot_in, "py")

    collect_planes(2, last_in)

    def out_block(i, carry):
        spectral = row_block(i)
        for g in range(4):
            o = 4 * i + g
            out_ref[o] = pre_ref[o] + spectral[32 * g : 32 * g + 32]
        return carry

    lax.fori_loop(0, groups, out_block, 0, unroll=4)

    bulk(9, slot_in, "py").wait_recv()
    for k in range(8):
        store_out_ref[k] = slot_in[:, 0, 32 * k : 32 * k + 32]
    for phase, dst, axis in (
        (0, piece_in, "py"),
        (1, chosen_in, "py"),
        (2, mixed_in, "py"),
        (3, plane_in, "px"),
        (4, part_in, "px"),
        (5, whole_in, "py"),
        (6, wall_in, "py"),
        (7, saved_in, "py"),
        (8, last_in, "px"),
        (9, slot_in, "py"),
    ):
        bulk(phase, dst, axis).wait_send()


def on_device(
    n_px,
    n_py,
    field_in,
    cotangent,
    spectrum_saved,
    weight_store,
    block_slot,
    kx_modes,
    ky_modes,
    pointwise,
    bias_vector,
):
    channels, _, rows_x, width_y = field_in.shape
    hbm = pl.BlockSpec(memory_space=pltpu.HBM)
    f32 = jnp.float32
    row = pltpu.VMEM((n_py, 1, 128), f32)
    tile = pltpu.VMEM((32, 128), f32)
    tiles = pltpu.VMEM((n_px, 32, 128), f32)
    field_grad, store_grad = pl.pallas_call(
        functools.partial(kernel, n_px, n_py),
        out_shape=(
            pltpu.VMEM((channels, rows_x, width_y), f32),
            pltpu.VMEM((8, channels, channels), f32),
        ),
        in_specs=[hbm] * 9,
        out_specs=(pl.BlockSpec(memory_space=pltpu.VMEM),) * 2,
        scratch_shapes=[
            pltpu.VMEM((channels, rows_x, width_y), jnp.bfloat16),
            pltpu.VMEM((channels, rows_x, width_y), jnp.bfloat16),
            pltpu.VMEM((channels, 2, 2, n_py), f32),
            pltpu.VMEM((8, channels, channels), f32),
            pltpu.VMEM((1, 2), jnp.int32),
            pltpu.VMEM((1, 32), jnp.int32),
            pltpu.VMEM((1, 32), jnp.int32),
            pltpu.VMEM((channels, channels), jnp.bfloat16),
            pltpu.VMEM((1, channels), f32),
            pltpu.VMEM((64, width_y), f32),
            pltpu.VMEM((channels, rows_x, width_y), f32),
            pltpu.VMEM((channels, rows_x, width_y), f32),
            pltpu.VMEM((n_px * 128, 128), f32),
            pltpu.VMEM((n_px * 128, 128), f32),
            pltpu.VMEM((n_py, 1, 384), f32),
            pltpu.VMEM((n_py, 1, 384), f32),
            row,
            row,
            row,
            row,
            tile,
            tiles,
            tiles,
            tiles,
            tiles,
            row,
            row,
            tile,
            pltpu.VMEM((n_py, 32, 128), f32),
            tile,
            tiles,
            tile,
            pltpu.VMEM((n_py, 32, 128), f32),
            pltpu.VMEM((2, 32, 128), f32),
            pltpu.VMEM((n_py, 1, 256), f32),
            pltpu.VMEM((n_py, 1, 256), f32),
            pltpu.SemaphoreType.DMA((10,)),
            pltpu.SemaphoreType.DMA((10,)),
            pltpu.SemaphoreType.DMA((3, n_px)),
            pltpu.SemaphoreType.DMA((n_px,)),
            pltpu.SemaphoreType.DMA((9,)),
        ],
        compiler_params=pltpu.CompilerParams(
            collective_id=0, has_side_effects=True, vmem_limit_bytes=48 << 20
        ),
    )(
        *held(
        field_in.reshape(channels, rows_x, width_y),
        cotangent.reshape(channels, rows_x, width_y),
        jnp.transpose(spectrum_saved[:, :, :, 0, :], (0, 2, 3, 1)),
        weight_store.reshape(8, channels, channels),
        block_slot,
        kx_modes.reshape(1, -1),
        ky_modes.reshape(1, -1),
        pointwise,
        bias_vector.reshape(1, -1),
            )
    )
    return (
        field_grad.reshape(field_in.shape),
        store_grad.reshape(weight_store.shape),
    )


def held(*arrays):
    return [pltpu.with_memory_space_constraint(array, pltpu.HBM) for array in arrays]


def solution(mesh):
    placed = (
        P(None, "py", "px", None),
        P(None, "py", "px", None),
        P(None, None, "px", "py", None),
        P(("px", "py"), None, None, None),
        P("py", "px"),
        P(),
        P(),
        P(),
        P(),
    )
    return jax.shard_map(
        functools.partial(on_device, mesh.shape["px"], mesh.shape["py"]),
        mesh=mesh,
        in_specs=placed,
        out_specs=(P(None, "py", "px", None), P(("px", "py"), None, None, None)),
        check_vma=False,
    )
```
